32 devices in a mesh: lat: 8 (over z, x), lev: 4 (over y, core).
Axes of the slice: x: 2, y: 2, z: 4, core: 2. Of those that a mesh axis runs over, the one named last changes fastest.
Arguments:
- fields: float32 [4, 64, 128, 1024], P(None, 'lat', 'lev'), may hold values from -6 to 6
- thickness: float32 [64, 128, 1024], P('lat', 'lev'), may hold values from 0.5 to 1.5
- courant_lon: float32 [64, 128, 1024], P('lat', 'lev'), may hold values from -0.8 to 0.8
- courant_lat: float32 [64, 128, 1024], P('lat', 'lev'), may hold values from -0.8 to 0.8
- exchange: float32 [2, 128, 128], replicated, may hold values from -0.5 to 0.5
- solar_profile: float32 [128], replicated, may hold values from 0.1 to 1
- owners: int32 [512, 1], P(('lat', 'lev')), may hold values from 0 to 7; in each aligned block of 16 rows (0 to 15, 16 to 31, ...) at most 2 rows name the same one
- daylight: int32 [512], P(('lat', 'lev')), may hold values 0 or 1
Outputs:
- remapped: float32 [4, 64, 128, 1024], P(None, 'lat', None, 'lev')
- heating: float32 [64, 128, 1024], P('lat', None, 'lev')
- owner_heat: float32 [8, 4], P('lat', 'lev')
The draws below stay inside these ranges and needn't reach their ends.
Inputs may be any that keep to these rules, and one draw needn't show every extreme that they name: `owners`: among the rows of one device at most 2 name the same owner.
All inputs are finite; a program needn't handle non-finite values. No bound on the sum of `daylight` on one device may be relied on, other than what follows from the above.
Results may differ from the reference program's by a relative error of at most 0.0003.
Values sent between devices are 32-bit elements; how exact they have to be, the bound alone decides.
A program may use at most 128 MiB of HBM per device.

```python
import math
import jax
import jax.numpy as jnp
import numpy as np
from jax import lax

NLON = 1024
NLEV = 128
FIELDS = 4
BANDS = 2
BLOCK_COLS = 128
CAP = 2
LAT_DEV = 8
NLAT = 64
PIECE = 256
NB = 16
BLOCKS = 512
OWNERS = 8
N_LAT = 8
N_LEV = 4


def place_ends(drawn, rng, low, high):
    longest = drawn.shape.index(max(drawn.shape))
    spots = []
    for shift in (0, 1):
        where = [jax.random.randint(jax.random.fold_in(rng, axis), (), 0, length) for axis, length in enumerate(drawn.shape)]
        where[longest] = (where[longest] + shift) % drawn.shape[longest]
        spots.append(tuple(where))
    return drawn.at[spots[0]].set(low).at[spots[1]].set(high)


def shard_levels(own_key, dims, split, smallest, largest):
    def one(axis_at, blocks):
        steps = jax.random.uniform(jax.random.fold_in(jax.random.fold_in(own_key, 6), axis_at), (blocks,), jnp.float32, smallest / len(split), largest / len(split))
        return jnp.repeat(jnp.exp(steps), dims[axis_at] // blocks).reshape((-1,) + (1,) * (len(dims) - axis_at - 1))

    level = one(*split[0])
    for cut in split[1:]:
        level = level * one(*cut)
    return level


def routed_block(key, own, number, rows, number_of, top, limit, skew):
    ranking = jax.random.permutation(key, number_of)
    crowded, usual = portions_of(number_of, rows * top, limit, skew, True), portions_of(number_of, rows * top, limit, skew, False)
    places = jnp.arange(number_of)

    def named(sizes, rotation):
        used = int((sizes > 0).sum())
        fixed = max(1, used // 4)
        passed = fixed + (places - fixed + rotation * (used - fixed)) % max(1, number_of - fixed)
        return jnp.zeros((number_of,), jnp.int32).at[ranking[jnp.where(places < fixed, places, passed)]].set(jnp.asarray(sizes, jnp.int32))

    sizes = jnp.where(number % 4 == 0, named(crowded, number // 4), named(usual, number - number // 4 - 1))
    mixed = jax.random.permutation(jax.random.fold_in(own, 3), number_of)
    source_of, taker = mixed[0:number_of // 2 * 2:2], mixed[1:number_of // 2 * 2:2]
    margin = jnp.minimum(sizes[source_of] - 1, limit - sizes[taker]) // 2
    margin = jnp.where((source_of == ranking[0]) | (taker == ranking[0]) | (sizes[taker] == 0), 0, jnp.maximum(margin, 0))
    passed = jax.random.randint(jax.random.fold_in(own, 4), (number_of // 2,), 0, 1 << 20) % (margin + 1)
    sizes = sizes.at[source_of].add(-passed).at[taker].add(passed)
    labels = jnp.searchsorted(jnp.cumsum(sizes), jnp.arange(rows * top), side="right").astype(jnp.int32)
    grid = labels.reshape(top, rows).T
    grid = grid[jax.random.permutation(jax.random.fold_in(own, 1), rows)]
    rotation = jax.random.randint(jax.random.fold_in(own, 2), (rows, 1), 0, top)
    return jnp.take_along_axis(grid, (jnp.arange(top)[None, :] + rotation) % top, axis=1)


def portions_of(amount, total, bound, lean, full):
    portions = [(1 << 20) // math.isqrt(grade ** lean) + 1 for grade in range(1, amount + 1)]
    largest = bound if full else min(bound, max(-(-total // amount), total * portions[0] // sum(portions)))
    least = 1 if total - largest >= amount - 1 else 0
    counts, surplus = [largest] + [least] * (amount - 1), total - largest - least * (amount - 1)
    while surplus > 0:
        free = [i for i in range(1, amount) if counts[i] < largest] or [i for i in range(1, amount) if counts[i] < bound]
        mass, left = sum([portions[i] for i in free]), surplus
        for i in free:
            extra = min(bound - counts[i], max(1, left * portions[i] // mass), surplus)
            counts[i] = counts[i] + extra
            surplus = surplus - extra
    return np.array(counts)


def noise(own_key, extent, deviation, limit, shards=(), kind=jnp.bfloat16):
    array = jax.random.normal(own_key, extent, jnp.float32) * deviation
    if len(shards) > 0:
        array = shard_levels(own_key, extent, shards, -0.22, 0.18) * array
    return jnp.clip(array, min=-limit, max=limit).astype(kind)


def setup_inputs(seed: int = 0) -> dict:
    streams_of = jax.random.split(jax.random.key(seed), 9)
    fields = noise(streams_of[0], (FIELDS, NLAT, NLEV, NLON), 1.0, 6.0, ((1, 8), (2, 4)), jnp.float32)
    thickness = jnp.clip(0.5 + 1.0 * jax.random.uniform(streams_of[1], (NLAT, NLEV, NLON), jnp.float32) ** shard_levels(streams_of[1], (NLAT, NLEV, NLON), ((0, 8), (1, 4)), -0.2, 0.2), 0.5, 1.5)
    courant_lon = jnp.clip(jax.random.uniform(streams_of[2], (NLAT, NLEV, NLON), jnp.float32, -0.8, 0.8) * shard_levels(streams_of[2], (NLAT, NLEV, NLON), ((0, 8), (1, 4)), -0.4, 0.0), -0.8, 0.8)
    courant_lat = jnp.clip(jax.random.uniform(streams_of[3], (NLAT, NLEV, NLON), jnp.float32, -0.8, 0.8) * shard_levels(streams_of[3], (NLAT, NLEV, NLON), ((0, 8), (1, 4)), -0.4, 0.0), -0.8, 0.8)
    exchange = noise(streams_of[4], (BANDS, NLEV, NLEV), NLEV ** -0.5, 0.5, (), jnp.float32)
    solar_profile = jnp.clip(jnp.exp(jax.random.uniform(streams_of[5], (NLEV,), jnp.float32, math.log(0.1), math.log(1.0))), 0.1, 1.0)
    owners_keys = jax.random.split(jax.random.fold_in(streams_of[6], 1), BLOCKS // NB)
    owners_turns = jax.random.permutation(jax.random.fold_in(streams_of[6], 3), BLOCKS // NB)
    owners = jax.vmap(lambda own, number: routed_block(jax.random.fold_in(streams_of[6], 2), own, number, NB, OWNERS, 1, CAP, 2))(owners_keys, owners_turns).reshape((BLOCKS, 1))
    daylight = place_ends((jax.random.randint(streams_of[7], (BLOCKS,), 0, 2) < 1).astype(jnp.int32), jax.random.fold_in(streams_of[7], 1), 0, 1)
    return dict(fields=fields, thickness=thickness, courant_lon=courant_lon, courant_lat=courant_lat, exchange=exchange, solar_profile=solar_profile, owners=owners, daylight=daylight)


HIGH = lax.Precision.HIGHEST


def wendroff(values, courant, plus, minus):
    return values - 0.5 * courant * (plus - minus) + 0.5 * courant * courant * (plus - 2.0 * values + minus)


def remap_row(row_fields, row_thick):
    levels = row_thick.shape[0]
    index = jnp.arange(levels)
    lower = (index[:, None] >= index[None, :]).astype(jnp.float32)
    upper_edge = jnp.dot(lower, row_thick, precision=HIGH, preferred_element_type=jnp.float32)
    lower_edge = upper_edge - row_thick
    spacing = upper_edge[-1] / levels
    steps_f = index.astype(jnp.float32)
    ref_lo = steps_f[:, None] * spacing[None, :]
    ref_hi = (steps_f + 1.0)[:, None] * spacing[None, :]
    intersection = jnp.maximum(jnp.minimum(ref_hi[:, None, :], upper_edge[None, :, :]) - jnp.maximum(ref_lo[:, None, :], lower_edge[None, :, :]), 0.0)
    mixed = jnp.einsum('ijc,fjc->fic', intersection, row_fields, precision=HIGH)
    return mixed / spacing[None, None, :]


def physics(temp, humid, day, exchange, solar, form):
    square = humid * humid
    absorb = square / (1.0 + square)
    clear = 1.0 / (1.0 + square)
    heat = jnp.einsum(form, exchange[0], absorb * temp, precision=HIGH)
    heat = heat + jnp.einsum(form, exchange[1], clear * temp, precision=HIGH)
    return heat + day * solar * clear


def reference(fields, thickness, courant_lon, courant_lat, exchange, solar_profile, owners, daylight):
    plus = jnp.roll(fields, -1, axis=3)
    minus = jnp.roll(fields, 1, axis=3)
    stepped = wendroff(fields, courant_lon[None], plus, minus)
    padded = jnp.pad(stepped, ((0, 0), (1, 1), (0, 0), (0, 0)))
    stepped = wendroff(stepped, courant_lat[None], padded[:, 2:], padded[:, :-2])

    def one_row(row):
        row_fields = lax.dynamic_index_in_dim(stepped, row, 1, keepdims=False)
        row_thick = lax.dynamic_index_in_dim(thickness, row, 0, keepdims=False)
        return remap_row(row_fields, row_thick)

    remapped = jnp.moveaxis(lax.map(one_row, jnp.arange(NLAT)), 0, 1)
    per_row = PIECE // BLOCK_COLS
    day_grid = daylight.reshape(N_LAT, N_LEV, LAT_DEV, per_row).transpose(0, 2, 1, 3).reshape(NLAT, N_LEV * per_row)
    day_cols = jnp.repeat(day_grid.astype(jnp.float32), BLOCK_COLS, axis=1)
    heat = physics(remapped[0], remapped[1], day_cols[:, None, :], exchange, solar_profile[:, None], 'ij,ajc->aic')
    means = jnp.sum(heat.reshape(NLAT, NLEV, N_LEV * per_row, BLOCK_COLS), axis=(1, 3)) / (NLEV * BLOCK_COLS)
    means = means.reshape(N_LAT, LAT_DEV, N_LEV, per_row).transpose(0, 2, 1, 3).reshape(N_LAT, N_LEV, NB)
    onehot = (owners[:, 0].reshape(N_LAT, N_LEV, NB)[..., None] == jnp.arange(OWNERS)[None, None, None, :]).astype(jnp.float32)
    owner_heat = jnp.sum(onehot * means[..., None], axis=(0, 2)).T
    return (remapped, heat, owner_heat)
```

```python
import functools

import jax
import jax.numpy as jnp
from jax import lax
from jax.experimental import pallas as pl
from jax.experimental.pallas import tpu as pltpu
from jax.sharding import PartitionSpec as P

BLOCK_COLS = 128
THIN, THICK = 0.5, 1.5
TILE = 16
STEP = 4
LONG = 8
LEAD = 2
HIGH = lax.Precision.HIGHEST
MESH = pl.DeviceIdType.MESH


def wendroff(values, half, half_square, plus, minus):
    return values - half * (plus - minus) + half_square * (plus - 2.0 * values + minus)


def layers_of(first, last, levels):
    def most(n):
        return levels * THICK * n / (THICK * n + THIN * (levels - n))

    def least(n):
        return levels * THIN * n / (THIN * n + THICK * (levels - n))

    slack = 0.01
    hit = [j for j in range(levels) if least(j) < last + slack and most(j + 1) > first - slack]
    return hit[0] // STEP * STEP, min(levels, -(-(hit[-1] + 1) // STEP) * STEP)


def remap(levels, spacing, upper, lower, value, count, put):
    inverse = 1.0 / spacing
    tile_line = lax.broadcasted_iota(jnp.int32, (TILE, BLOCK_COLS), 0).astype(jnp.float32)
    for i in range(0, levels, TILE):
        low = (tile_line + float(i)) * spacing
        high = (tile_line + float(i + 1)) * spacing
        first, last = layers_of(i, i + TILE, levels)

        def add(j0, steps, sums, low=low, high=high):
            for s in range(steps):
                j = pl.ds(j0 + s, 1)
                shared = jnp.maximum(
                    jnp.minimum(high, upper(j)) - jnp.maximum(low, lower(j)), 0.0
                )
                sums = tuple(total + shared * value(f, j) for f, total in enumerate(sums))
            return sums

        def add_long(g, sums, add=add, first=first):
            return add(first + g * LONG, LONG, sums)

        trips, rest = divmod(last - first, LONG)
        sums = (jnp.zeros((TILE, BLOCK_COLS), jnp.float32),) * count
        sums = lax.fori_loop(0, trips, add_long, sums)
        if rest:
            sums = add(last - rest, rest, sums)
        for f in range(count):
            put(f, i, sums[f] * inverse)


def kernel(
    n_lat, n_lev,
    fields, thickness, courant_lon, courant_lat, exchange, solar, owners, daylight,
    out, heating, owner_heat, final, final_edges,
    fbuf, lonbuf, latbuf, stp, sbuf, rbuf, tbuf, matrix, sunbuf, upper, lower, shares, gathered,
    go, lat_go,
    in_sem, lat_in_sem, small_sem, halo_send, halo_recv, thick_send, thick_recv, thick_own,
    send_sem, recv_sem, own_sem, share_send, share_recv,
):
    count, rows, depth, width = fields.shape
    levels = out.shape[2]
    piece = width // n_lev
    per_row = piece // BLOCK_COLS
    groups = count // LEAD
    tail = 2 * per_row
    lat = lax.axis_index("lat")
    lev = lax.axis_index("lev")
    odd = lax.rem(lev, 2) == 1
    even = jnp.logical_not(odd)
    partner = lev + 1 - 2 * lax.rem(lev, 2)

    barrier = pltpu.get_barrier_semaphore()
    for d in range(1, n_lev):
        peer = lax.rem(lev + d, n_lev)

        @pl.when(lax.rem(peer, 2) == 0)
        def _():
            pl.semaphore_signal(barrier, inc=1, device_id={"lev": peer}, device_id_type=MESH)

    def load(r):
        return (
            pltpu.make_async_copy(fields.at[:, r], fbuf.at[:, r], in_sem.at[r, 0]),
            pltpu.make_async_copy(courant_lon.at[r], lonbuf.at[r], in_sem.at[r, 1]),
        )

    for k in range(rows):
        for copy in load((k + rows - 1) % rows):
            copy.start()
    lat_load = pltpu.make_async_copy(courant_lat, latbuf, lat_in_sem)
    lat_load.start()
    bands = exchange.shape[0]
    small_loads = [
        pltpu.make_async_copy(
            exchange.at[k], matrix.at[:, pl.ds(k * levels, levels)], small_sem.at[k]
        )
        for k in range(bands)
    ] + [pltpu.make_async_copy(solar, sunbuf, small_sem.at[bands])]
    for copy in small_loads:
        copy.start()

    def span(index, size):
        return pl.ds(pl.multiple_of(index * size, size), size)

    own_thick = pltpu.make_async_copy(
        thickness.at[:, :, span(lev, piece)], tbuf.at[:, span(lev, depth)], thick_own
    )
    own_thick.start()

    @pl.when(even)
    def _():
        pl.semaphore_wait(barrier, n_lev - 1)
        pl.semaphore_signal(go, inc=1, device_id={"lev": partner}, device_id_type=MESH)

    @pl.when(odd)
    def _():
        pl.semaphore_wait(go, 1)

        @pl.loop(1, n_lat)
        def _(d):
            pl.semaphore_signal(
                barrier, inc=1, device_id={"lat": lax.rem(lat + d, n_lat)}, device_id_type=MESH
            )

    def wait_for_lat():
        @pl.when(odd)
        def _():
            pl.semaphore_wait(barrier, n_lat - 1)
            pl.semaphore_signal(lat_go, inc=1, device_id={"lev": partner}, device_id_type=MESH)

        @pl.when(even)
        def _():
            pl.semaphore_wait(lat_go, 1)

    def thick_copy(r, d, source):
        target = lax.rem(lev + d, n_lev)
        return pltpu.make_async_remote_copy(
            src_ref=thickness.at[r, :, span(target, piece)],
            dst_ref=tbuf.at[r, span(source, depth)],
            send_sem=thick_send.at[r, d],
            recv_sem=thick_recv.at[r, d],
            device_id={"lev": target},
            device_id_type=MESH,
        )

    @pl.loop(1, rows + 1)
    def _(k):
        for d in range(1, n_lev):
            thick_copy(lax.rem(k, rows), d, lev).start()

    def lon_row(r):
        for copy in load(r):
            copy.wait()

        @pl.loop(0, depth // 8)
        def _(g):
            part = span(g, 8)
            c = lonbuf[r, part, :]
            half, half_square = 0.5 * c, 0.5 * c * c
            for f in range(count):
                q = fbuf[f, r, part, :]
                plus = pltpu.roll(q, width - 1, 1)
                minus = pltpu.roll(q, 1, 1)
                stp[f, r + 1, part, :] = wendroff(q, half, half_square, plus, minus)

    def halo(way):
        source, target = (rows, 0) if way == 0 else (1, rows + 1)
        return pltpu.make_async_remote_copy(
            src_ref=stp.at[:, source],
            dst_ref=stp.at[:, target],
            send_sem=halo_send.at[way],
            recv_sem=halo_recv.at[way],
            device_id={"lat": lax.rem(lat + (1 if way == 0 else n_lat - 1), n_lat)},
            device_id_type=MESH,
        )

    has_next = lat < n_lat - 1
    has_last = lat > 0

    @pl.loop(0, rows)
    def _(k):
        lon_row(lax.rem(k + rows - 1, rows))

    lat_load.wait()

    def piece_copy(r, b, d, source, group=None):
        target = lax.rem(lev + d, n_lev)
        picked = pl.ds(0, count) if group is None else span(group, LEAD)
        at = 0 if group is None else group
        return pltpu.make_async_remote_copy(
            src_ref=sbuf.at[target, r, b, picked],
            dst_ref=rbuf.at[r, b, picked, span(source, depth)],
            send_sem=send_sem.at[r, b, at, d],
            recv_sem=recv_sem.at[r, b, at, d],
            device_id={"lev": target},
            device_id_type=MESH,
        )

    def own_copy(r, b):
        return pltpu.make_async_copy(
            sbuf.at[lev, r, b], rbuf.at[r, b, :, span(lev, depth)], own_sem.at[r, b]
        )

    def lat_row(r):
        @pl.loop(0, depth // 8)
        def _(g):
            part = span(g, 8)
            c = latbuf[r, part, :]
            half, half_square = 0.5 * c, 0.5 * c * c
            for f in range(count):
                moved = wendroff(
                    stp[f, r + 1, part, :], half, half_square,
                    stp[f, r + 2, part, :], stp[f, r, part, :],
                )
                for p in range(n_lev):
                    for b in range(per_row):
                        at = p * piece + b * BLOCK_COLS
                        sbuf[p, r, b, f, part, :] = moved[:, at:at + BLOCK_COLS]

    def send_row(r, group=None):
        for b in range(per_row):
            for d in range(1, n_lev):
                piece_copy(r, b, d, lev, group).start()

    def own_row(r):
        for b in range(per_row):
            own_copy(r, b).start()

    @pl.loop(1, rows - 1)
    def _(r):
        lat_row(r)
        send_row(r)
        own_row(r)

    wait_for_lat()

    @pl.when(has_next)
    def _():
        halo(0).start()

    @pl.when(has_last)
    def _():
        halo(1).start()

    @pl.when(jnp.logical_not(has_last))
    def _():
        stp[:, 0] = jnp.zeros((count, depth, width), jnp.float32)

    @pl.when(jnp.logical_not(has_next))
    def _():
        stp[:, rows + 1] = jnp.zeros((count, depth, width), jnp.float32)

    for copy in small_loads:
        copy.wait()
    line = lax.broadcasted_iota(jnp.int32, (levels, levels), 0)
    column = lax.broadcasted_iota(jnp.int32, (levels, levels), 1)
    sun = jnp.sum(
        jnp.where(line == column, jnp.broadcast_to(sunbuf[...], (levels, levels)), 0.0),
        axis=1, keepdims=True,
    )
    triangle = (line >= column).astype(jnp.float32)
    lanes = lax.broadcasted_iota(jnp.int32, (1, BLOCK_COLS), 1)
    shares[...] = jnp.zeros_like(shares)

    own_thick.wait()

    def source_of(d):
        return lax.rem(lev + n_lev - d, n_lev)

    @pl.loop(1, rows + 1)
    def _(k):
        r = lax.rem(k, rows)
        for d in range(1, n_lev):
            thick_copy(r, d, source_of(d)).wait_recv()
        thick = tbuf[r]
        edge = jnp.dot(triangle, thick, precision=HIGH, preferred_element_type=jnp.float32)
        for b in range(per_row):
            cols = slice(b * BLOCK_COLS, (b + 1) * BLOCK_COLS)
            upper[r, b] = edge[:, cols]
            lower[r, b] = edge[:, cols] - thick[:, cols]

    def spacing_of(r, b):
        return upper[r, b, levels - 1:levels, :] / levels

    def remap_block(r, b, base, some):
        cols = span(b, BLOCK_COLS)

        def put(f, i, tile):
            out[base + f, r, i:i + TILE, cols] = tile

        remap(
            levels, spacing_of(r, b), lambda j: upper[r, b, j, :], lambda j: lower[r, b, j, :],
            lambda f, j: rbuf[r, b, base + f, j, :], some, put,
        )

    def heat_block(r, b):
        cols = span(b, BLOCK_COLS)
        temp, humid = out[0, r, :, cols], out[1, r, :, cols]
        square = humid * humid
        clear = 1.0 / (1.0 + square)
        heat = jnp.dot(
            matrix[...], jnp.concatenate([square * clear * temp, clear * temp], axis=0),
            precision=HIGH, preferred_element_type=jnp.float32,
        )
        block = r * per_row + b
        warm = heat + daylight[block].astype(jnp.float32) * sun * clear
        heating[r, :, cols] = warm
        mean = jnp.sum(jnp.sum(warm, axis=0, keepdims=True), axis=1, keepdims=True)
        mean = mean * (1.0 / (levels * BLOCK_COLS))
        shares[...] = shares[...] + jnp.where(lanes == owners[block], mean, 0.0)

    def share_copy(d, slot):
        return pltpu.make_async_remote_copy(
            src_ref=shares,
            dst_ref=gathered.at[slot],
            send_sem=share_send.at[d],
            recv_sem=share_recv.at[d],
            device_id={"lat": lax.rem(lat + d, n_lat)},
            device_id_type=MESH,
        )

    @pl.loop(0, (rows - 2) * per_row)
    def _(c):
        b = lax.rem(c, per_row)
        r = c // per_row + 1

        @pl.when(c == min(3, rows - 3) * per_row)
        def _():
            @pl.when(has_last)
            def _():
                halo(0).wait_recv()

            @pl.when(has_next)
            def _():
                halo(1).wait_recv()

            lat_row(rows - 1)
            send_row(rows - 1, 0)
            lat_row(0)
            send_row(0, 0)
            for group in range(1, groups):
                send_row(rows - 1, group)
                send_row(0, group)
            own_row(rows - 1)
            own_row(0)

        own_copy(r, b).wait()
        for d in range(1, n_lev):
            piece_copy(r, b, d, source_of(d)).wait_recv()
        remap_block(r, b, 0, count)
        heat_block(r, b)

    def tail_block(t):
        at = lax.rem(t, tail)
        return lax.rem(rows - 1 + at // per_row, rows), lax.rem(at, per_row), t // tail

    @pl.loop(0, groups * tail - 1)
    def _(t):
        r, b, group = tail_block(t)

        @pl.when(group == 0)
        def _():
            own_copy(r, b).wait()

        for d in range(1, n_lev):
            piece_copy(r, b, d, source_of(d), group).wait_recv()
        remap_block(r, b, group * LEAD, LEAD)

        @pl.when(group == 0)
        def _():
            heat_block(r, b)

        @pl.when(t == tail - 1)
        def _():
            @pl.loop(1, n_lat)
            def _(d):
                share_copy(d, d).start()

    end = per_row - 1
    final_edges[0] = upper[0, end]
    final_edges[1] = lower[0, end]

    @pl.loop(0, rows)
    def _(r):
        for d in range(1, n_lev):
            thick_copy(r, d, lev).wait_send()

    @pl.loop(1, rows - 1)
    def _(r):
        for b in range(per_row):
            for d in range(1, n_lev):
                piece_copy(r, b, d, lev).wait_send()

    @pl.when(has_next)
    def _():
        halo(0).wait_send()

    @pl.when(has_last)
    def _():
        halo(1).wait_send()

    def collect(d, total):
        share_copy(d, d).wait_recv()
        return total + gathered[d]

    total = lax.fori_loop(1, n_lat, collect, shares[...])
    owner_heat[...] = jnp.sum(
        jnp.where(lanes == lat, total, 0.0), axis=1, keepdims=True
    )

    @pl.loop(1, n_lat)
    def _(d):
        share_copy(d, d).wait_send()

    @pl.loop(0, groups * tail)
    def _(t):
        r, b, group = tail_block(t)
        for d in range(1, n_lev):
            piece_copy(r, b, d, lev, group).wait_send()

    for d in range(1, n_lev):
        piece_copy(0, end, d, source_of(d), groups - 1).wait_recv()
    final[...] = rbuf[0, end, (groups - 1) * LEAD:groups * LEAD]


def store(
    moved, warm, owner, final, edges, out, heating, owner_heat, tile, sems,
):
    count, rows, levels, piece = moved.shape
    rest = piece - BLOCK_COLS
    kept = count - LEAD
    pairs = [(moved.at[:, r], out.at[:, r]) for r in range(1, rows)] + [
        (warm, heating),
        (owner, owner_heat),
        (moved.at[pl.ds(0, kept), 0], out.at[pl.ds(0, kept), 0]),
    ]
    if rest:
        pairs.append((
            moved.at[pl.ds(kept, LEAD), 0, :, pl.ds(0, rest)],
            out.at[pl.ds(kept, LEAD), 0, :, pl.ds(0, rest)],
        ))
    copies = [
        pltpu.make_async_copy(source, target, sems.at[k])
        for k, (source, target) in enumerate(pairs)
    ]
    for copy in copies:
        copy.start()

    def put(f, i, value):
        tile[f, i:i + TILE, :] = value

    remap(
        levels, edges[0, levels - 1:levels, :] / levels,
        lambda j: edges[0, j, :], lambda j: edges[1, j, :], lambda f, j: final[f, j, :], LEAD, put,
    )
    last = pltpu.make_async_copy(
        tile, out.at[pl.ds(kept, LEAD), 0, :, pl.ds(rest, BLOCK_COLS)], sems.at[len(pairs)]
    )
    last.start()
    for copy in copies:
        copy.wait()
    last.wait()


def per_device(
    fields, thickness, courant_lon, courant_lat, exchange, solar_profile, owners, daylight
):
    n_lat, n_lev = lax.axis_size("lat"), lax.axis_size("lev")
    count, rows, depth, width = fields.shape
    levels = solar_profile.shape[0]
    piece = width // n_lev
    per_row = piece // BLOCK_COLS
    groups = count // LEAD
    bands = exchange.shape[0]
    f32 = jnp.float32
    dma = pltpu.SemaphoreType.DMA
    regular = pltpu.SemaphoreType.REGULAR
    hbm = pl.BlockSpec(memory_space=pltpu.HBM)
    vmem = pl.BlockSpec(memory_space=pltpu.VMEM)
    smem = pl.BlockSpec(memory_space=pltpu.SMEM)
    moved = jax.ShapeDtypeStruct((count, rows, levels, piece), f32)
    warm = jax.ShapeDtypeStruct((rows, levels, piece), f32)
    owner = jax.ShapeDtypeStruct((1, 1), f32)
    results = pl.pallas_call(
        functools.partial(kernel, n_lat, n_lev),
        out_shape=(
            pltpu.VMEM(moved.shape, f32),
            pltpu.VMEM(warm.shape, f32),
            pltpu.VMEM(owner.shape, f32),
            pltpu.VMEM((LEAD, levels, BLOCK_COLS), f32),
            pltpu.VMEM((2, levels, BLOCK_COLS), f32),
        ),
        in_specs=[hbm, hbm, hbm, hbm, hbm, hbm, smem, smem],
        out_specs=(vmem,) * 5,
        scratch_shapes=[
            pltpu.VMEM((count, rows, depth, width), f32),
            pltpu.VMEM((rows, depth, width), f32),
            pltpu.VMEM((rows, depth, width), f32),
            pltpu.VMEM((count, rows + 2, depth, width), f32),
            pltpu.VMEM((n_lev, rows, per_row, count, depth, BLOCK_COLS), f32),
            pltpu.VMEM((rows, per_row, count, levels, BLOCK_COLS), f32),
            pltpu.VMEM((rows, levels, piece), f32),
            pltpu.VMEM((levels, bands * levels), f32),
            pltpu.VMEM((1, levels), f32),
            pltpu.VMEM((rows, per_row, levels, BLOCK_COLS), f32),
            pltpu.VMEM((rows, per_row, levels, BLOCK_COLS), f32),
            pltpu.VMEM((1, BLOCK_COLS), f32),
            pltpu.VMEM((n_lat, 1, BLOCK_COLS), f32),
            regular,
            regular,
            dma((rows, 2)),
            dma,
            dma((bands + 1,)),
            dma((2,)),
            dma((2,)),
            dma((rows, n_lev)),
            dma((rows, n_lev)),
            dma,
            dma((rows, per_row, groups, n_lev)),
            dma((rows, per_row, groups, n_lev)),
            dma((rows, per_row)),
            dma((n_lat,)),
            dma((n_lat,)),
        ],
        compiler_params=pltpu.CompilerParams(
            collective_id=0, has_side_effects=True, vmem_limit_bytes=61400000
        ),
    )(
        fields, thickness, courant_lon, courant_lat, exchange, solar_profile[None, :],
        owners[:, 0], daylight,
    )
    return pl.pallas_call(
        store,
        out_shape=(moved, warm, owner),
        in_specs=[vmem] * 5,
        out_specs=(hbm,) * 3,
        scratch_shapes=[pltpu.VMEM((LEAD, levels, BLOCK_COLS), f32), dma((rows + 4,))],
        compiler_params=pltpu.CompilerParams(vmem_limit_bytes=12 * 1024 * 1024),
    )(*results)


def solution(mesh):
    placed = (
        P(None, "lat", "lev", None),
        P("lat", "lev", None),
        P("lat", "lev", None),
        P("lat", "lev", None),
        P(),
        P(),
        P(("lat", "lev"), None),
        P(("lat", "lev")),
    )
    return jax.shard_map(
        per_device,
        mesh=mesh,
        in_specs=placed,
        out_specs=(P(None, "lat", None, "lev"), P("lat", None, "lev"), P("lat", "lev")),
        check_vma=False,
    )
```

```python
import functools

import jax
import jax.numpy as jnp
from jax import lax
from jax.experimental import pallas as pl
from jax.experimental.pallas import tpu as pltpu
from jax.sharding import PartitionSpec as P

BLOCK_COLS = 128
THIN, THICK = 0.5, 1.5
TILE = 16
STEP = 4
LONG = 8
LEAD = 2
HIGH = lax.Precision.HIGHEST
MESH = pl.DeviceIdType.MESH


def wendroff(values, half, half_square, plus, minus):
    return values - half * (plus - minus) + half_square * (plus - 2.0 * values + minus)


def layers_of(first, last, levels):
    def most(n):
        return levels * THICK * n / (THICK * n + THIN * (levels - n))

    def least(n):
        return levels * THIN * n / (THIN * n + THICK * (levels - n))

    slack = 0.01
    hit = [j for j in range(levels) if least(j) < last + slack and most(j + 1) > first - slack]
    return hit[0] // STEP * STEP, min(levels, -(-(hit[-1] + 1) // STEP) * STEP)


def remap(levels, spacing, upper, lower, value, count, put):
    inverse = 1.0 / spacing
    tile_line = lax.broadcasted_iota(jnp.int32, (TILE, BLOCK_COLS), 0).astype(jnp.float32)
    for i in range(0, levels, TILE):
        low = (tile_line + float(i)) * spacing
        high = (tile_line + float(i + 1)) * spacing
        first, last = layers_of(i, i + TILE, levels)

        def add(j0, steps, sums, low=low, high=high):
            for s in range(steps):
                j = pl.ds(j0 + s, 1)
                shared = jnp.maximum(
                    jnp.minimum(high, upper(j)) - jnp.maximum(low, lower(j)), 0.0
                )
                sums = tuple(total + shared * value(f, j) for f, total in enumerate(sums))
            return sums

        def add_long(g, sums, add=add, first=first):
            return add(first + g * LONG, LONG, sums)

        trips, rest = divmod(last - first, LONG)
        sums = (jnp.zeros((TILE, BLOCK_COLS), jnp.float32),) * count
        sums = lax.fori_loop(0, trips, add_long, sums)
        if rest:
            sums = add(last - rest, rest, sums)
        for f in range(count):
            put(f, i, sums[f] * inverse)


def kernel(
    n_lat, n_lev,
    fields, thickness, courant_lon, courant_lat, exchange, solar, owners, daylight,
    out, heating, owner_heat, final, final_edges,
    fbuf, latbuf, stp, sbuf, rbuf, tbuf, matrix, sunbuf, upper, lower, shares, gathered,
    owner_of, day_of, go, lat_go,
    in_sem, lat_in_sem, small_sem, halo_send, halo_recv, thick_send, thick_recv,
    send_sem, recv_sem, share_send, share_recv,
):
    count, rows, depth, width = fields.shape
    levels = out.shape[2]
    piece = width // n_lev
    per_row = piece // BLOCK_COLS
    groups = count // LEAD
    tail = 2 * per_row
    lat = lax.axis_index("lat")
    lev = lax.axis_index("lev")
    odd = lax.rem(lev, 2) == 1
    even = jnp.logical_not(odd)
    partner = lev + 1 - 2 * lax.rem(lev, 2)

    barrier = pltpu.get_barrier_semaphore()
    for d in range(1, n_lev):
        peer = lax.rem(lev + d, n_lev)

        @pl.when(lax.rem(peer, 2) == 0)
        def _():
            pl.semaphore_signal(barrier, inc=1, device_id={"lev": peer}, device_id_type=MESH)

    def load(r):
        return (
            pltpu.make_async_copy(fields.at[:, r], fbuf.at[pl.ds(0, count), r], in_sem.at[r]),
            pltpu.make_async_copy(courant_lon.at[r], fbuf.at[count, r], in_sem.at[r]),
        )

    for k in range(rows):
        for copy in load((k + rows - 1) % rows):
            copy.start()
    lat_load = pltpu.make_async_copy(courant_lat, latbuf, lat_in_sem)
    lat_load.start()
    small = ((exchange, matrix), (solar, sunbuf), (owners, owner_of), (daylight, day_of))
    small_loads = [
        pltpu.make_async_copy(source, target, small_sem.at[k])
        for k, (source, target) in enumerate(small)
    ]
    for copy in small_loads:
        copy.start()

    def span(index, size):
        return pl.ds(pl.multiple_of(index * size, size), size)

    def landed(buffer, sem):
        pltpu.make_async_copy(buffer, buffer, sem).wait()

    @pl.loop(0, rows)
    def _(r):
        pltpu.make_async_copy(
            thickness.at[r, :, span(lev, piece)], tbuf.at[r, span(lev, depth)], thick_recv.at[r]
        ).start()

    @pl.when(even)
    def _():
        pl.semaphore_wait(barrier, n_lev - 1)
        pl.semaphore_signal(go, inc=1, device_id={"lev": partner}, device_id_type=MESH)

    @pl.when(odd)
    def _():
        pl.semaphore_wait(go, 1)

        @pl.loop(1, n_lat)
        def _(d):
            pl.semaphore_signal(
                barrier, inc=1, device_id={"lat": lax.rem(lat + d, n_lat)}, device_id_type=MESH
            )

    def wait_for_lat():
        @pl.when(odd)
        def _():
            pl.semaphore_wait(barrier, n_lat - 1)
            pl.semaphore_signal(lat_go, inc=1, device_id={"lev": partner}, device_id_type=MESH)

        @pl.when(even)
        def _():
            pl.semaphore_wait(lat_go, 1)

    def thick_copy(r, d):
        target = lax.rem(lev + d, n_lev)
        return pltpu.make_async_remote_copy(
            src_ref=thickness.at[r, :, span(target, piece)],
            dst_ref=tbuf.at[r, span(lev, depth)],
            send_sem=thick_send,
            recv_sem=thick_recv.at[r],
            device_id={"lev": target},
            device_id_type=MESH,
        )

    @pl.loop(1, rows + 1)
    def _(k):
        for d in range(1, n_lev):
            thick_copy(lax.rem(k, rows), d).start()

    def lon_row(r):
        landed(fbuf.at[:, r], in_sem.at[r])

        @pl.loop(0, depth // 8)
        def _(g):
            part = span(g, 8)
            c = fbuf[count, r, part, :]
            half, half_square = 0.5 * c, 0.5 * c * c
            for f in range(count):
                q = fbuf[f, r, part, :]
                plus = pltpu.roll(q, width - 1, 1)
                minus = pltpu.roll(q, 1, 1)
                stp[f, r + 1, part, :] = wendroff(q, half, half_square, plus, minus)

    def halo(way):
        source, target = (rows, 0) if way == 0 else (1, rows + 1)
        return pltpu.make_async_remote_copy(
            src_ref=stp.at[:, source],
            dst_ref=stp.at[:, target],
            send_sem=halo_send.at[way],
            recv_sem=halo_recv.at[way],
            device_id={"lat": lax.rem(lat + (1 if way == 0 else n_lat - 1), n_lat)},
            device_id_type=MESH,
        )

    has_next = lat < n_lat - 1
    has_last = lat > 0

    @pl.loop(0, rows)
    def _(k):
        lon_row(lax.rem(k + rows - 1, rows))

    lat_load.wait()

    def picked(group):
        return pl.ds(0, count) if group is None else span(group, LEAD)

    def slot(r, b, group):
        if group is None:
            return (r - 1) * per_row + b
        return (rows - 2) * per_row + group * tail + lax.rem(r + 1, rows) * per_row + b

    def piece_copy(r, b, d, group):
        target = lax.rem(lev + d, n_lev)
        return pltpu.make_async_remote_copy(
            src_ref=sbuf.at[target, r, b, picked(group)],
            dst_ref=rbuf.at[r, b, picked(group), span(lev, depth)],
            send_sem=send_sem.at[r],
            recv_sem=recv_sem.at[slot(r, b, group)],
            device_id={"lev": target},
            device_id_type=MESH,
        )

    def wait_piece(r, b, group=None):
        landed(rbuf.at[r, b, picked(group)], recv_sem.at[slot(r, b, group)])

    def lat_row(r):
        @pl.loop(0, depth // 8)
        def _(g):
            part = span(g, 8)
            c = latbuf[r, part, :]
            half, half_square = 0.5 * c, 0.5 * c * c
            for f in range(count):
                moved = wendroff(
                    stp[f, r + 1, part, :], half, half_square,
                    stp[f, r + 2, part, :], stp[f, r, part, :],
                )
                for p in range(n_lev):
                    for b in range(per_row):
                        at = p * piece + b * BLOCK_COLS
                        sbuf[p, r, b, f, part, :] = moved[:, at:at + BLOCK_COLS]

    def send_row(r, group=None):
        for b in range(per_row):
            for d in range(1, n_lev):
                piece_copy(r, b, d, group).start()
        for b in range(per_row):
            pltpu.make_async_copy(
                sbuf.at[lev, r, b, picked(group)],
                rbuf.at[r, b, picked(group), span(lev, depth)],
                recv_sem.at[slot(r, b, group)],
            ).start()

    @pl.loop(1, rows - 1)
    def _(r):
        lat_row(r)
        send_row(r)

    wait_for_lat()

    @pl.when(has_next)
    def _():
        halo(0).start()

    @pl.when(has_last)
    def _():
        halo(1).start()

    @pl.when(jnp.logical_not(has_last))
    def _():
        stp[:, 0] = jnp.zeros((count, depth, width), jnp.float32)

    @pl.when(jnp.logical_not(has_next))
    def _():
        stp[:, rows + 1] = jnp.zeros((count, depth, width), jnp.float32)

    for copy in small_loads:
        copy.wait()
    line = lax.broadcasted_iota(jnp.int32, (levels, levels), 0)
    column = lax.broadcasted_iota(jnp.int32, (levels, levels), 1)
    sun = jnp.sum(
        jnp.where(line == column, jnp.broadcast_to(sunbuf[...], (levels, levels)), 0.0),
        axis=1, keepdims=True,
    )
    triangle = (line >= column).astype(jnp.float32)
    lanes = lax.broadcasted_iota(jnp.int32, (1, BLOCK_COLS), 1)
    shares[...] = jnp.zeros_like(shares)

    @pl.loop(1, rows + 1)
    def _(k):
        r = lax.rem(k, rows)
        landed(tbuf.at[r], thick_recv.at[r])
        thick = tbuf[r]
        edge = jnp.dot(triangle, thick, precision=HIGH, preferred_element_type=jnp.float32)
        for b in range(per_row):
            cols = slice(b * BLOCK_COLS, (b + 1) * BLOCK_COLS)
            upper[r, b] = edge[:, cols]
            lower[r, b] = edge[:, cols] - thick[:, cols]

    def spacing_of(r, b):
        return upper[r, b, levels - 1:levels, :] / levels

    def remap_block(r, b, base, some):
        cols = span(b, BLOCK_COLS)

        def put(f, i, tile):
            out[base + f, r, i:i + TILE, cols] = tile

        remap(
            levels, spacing_of(r, b), lambda j: upper[r, b, j, :], lambda j: lower[r, b, j, :],
            lambda f, j: rbuf[r, b, base + f, j, :], some, put,
        )

    def heat_block(r, b):
        cols = span(b, BLOCK_COLS)
        temp, humid = out[0, r, :, cols], out[1, r, :, cols]
        square = humid * humid
        clear = 1.0 / (1.0 + square)
        heat = jnp.dot(
            jnp.concatenate([matrix[k] for k in range(matrix.shape[0])], axis=1),
            jnp.concatenate([square * clear * temp, clear * temp], axis=0),
            precision=HIGH, preferred_element_type=jnp.float32,
        )
        block = r * per_row + b
        warm = heat + day_of[block].astype(jnp.float32) * sun * clear
        heating[r, :, cols] = warm
        mean = jnp.sum(jnp.sum(warm, axis=0, keepdims=True), axis=1, keepdims=True)
        mean = mean * (1.0 / (levels * BLOCK_COLS))
        shares[...] = shares[...] + jnp.where(lanes == owner_of[block], mean, 0.0)

    def share_copy(d):
        return pltpu.make_async_remote_copy(
            src_ref=shares,
            dst_ref=gathered.at[d],
            send_sem=share_send,
            recv_sem=share_recv,
            device_id={"lat": lax.rem(lat + d, n_lat)},
            device_id_type=MESH,
        )

    @pl.loop(0, (rows - 2) * per_row)
    def _(c):
        b = lax.rem(c, per_row)
        r = c // per_row + 1

        @pl.when(c == min(3, rows - 3) * per_row)
        def _():
            @pl.when(has_last)
            def _():
                halo(0).wait_recv()

            @pl.when(has_next)
            def _():
                halo(1).wait_recv()

            lat_row(rows - 1)
            send_row(rows - 1, 0)
            lat_row(0)
            send_row(0, 0)
            for group in range(1, groups):
                send_row(rows - 1, group)
                send_row(0, group)

        wait_piece(r, b)
        remap_block(r, b, 0, count)
        heat_block(r, b)

    def tail_block(t):
        at = lax.rem(t, tail)
        return lax.rem(rows - 1 + at // per_row, rows), lax.rem(at, per_row), t // tail

    @pl.loop(0, groups * tail - 1)
    def _(t):
        r, b, group = tail_block(t)

        wait_piece(r, b, group)
        remap_block(r, b, group * LEAD, LEAD)

        @pl.when(group == 0)
        def _():
            heat_block(r, b)

        @pl.when(t == tail - 1)
        def _():
            @pl.loop(1, n_lat)
            def _(d):
                share_copy(d).start()

    end = per_row - 1
    final_edges[0] = upper[0, end]
    final_edges[1] = lower[0, end]

    landed(tbuf.at[:, pl.ds(0, depth * (n_lev - 1))], thick_send)

    @pl.when(has_next)
    def _():
        halo(0).wait_send()

    @pl.when(has_last)
    def _():
        halo(1).wait_send()

    others = gathered.at[pl.ds(1, n_lat - 1)]
    landed(others, share_recv)
    total = lax.fori_loop(1, n_lat, lambda d, total: total + gathered[d], shares[...])
    owner_heat[...] = jnp.sum(
        jnp.where(lanes == lat, total, 0.0), axis=1, keepdims=True
    )
    landed(others, share_send)

    @pl.loop(0, rows)
    def _(r):
        landed(sbuf.at[pl.ds(0, n_lev - 1), r], send_sem.at[r])

    wait_piece(0, end, groups - 1)
    final[...] = rbuf[0, end, (groups - 1) * LEAD:groups * LEAD]


def store(
    moved, warm, owner, final, edges, out, heating, owner_heat, tile, sems,
):
    count, rows, levels, piece = moved.shape
    rest = piece - BLOCK_COLS
    kept = count - LEAD
    inner = pl.ds(1, rows - 1)
    pairs = [
        (moved.at[:, inner], out.at[:, inner]),
        (warm, heating),
        (owner, owner_heat),
        (moved.at[pl.ds(0, kept), 0], out.at[pl.ds(0, kept), 0]),
    ]
    if rest:
        pairs.append((
            moved.at[pl.ds(kept, LEAD), 0, :, pl.ds(0, rest)],
            out.at[pl.ds(kept, LEAD), 0, :, pl.ds(0, rest)],
        ))
    copies = [
        pltpu.make_async_copy(source, target, sems.at[k])
        for k, (source, target) in enumerate(pairs)
    ]
    for copy in copies:
        copy.start()

    def put(f, i, value):
        tile[f, i:i + TILE, :] = value

    remap(
        levels, edges[0, levels - 1:levels, :] / levels,
        lambda j: edges[0, j, :], lambda j: edges[1, j, :], lambda f, j: final[f, j, :], LEAD, put,
    )
    last = pltpu.make_async_copy(
        tile, out.at[pl.ds(kept, LEAD), 0, :, pl.ds(rest, BLOCK_COLS)], sems.at[len(pairs)]
    )
    last.start()
    for copy in copies:
        copy.wait()
    last.wait()


def per_device(
    fields, thickness, courant_lon, courant_lat, exchange, solar_profile, owners, daylight
):
    n_lat, n_lev = lax.axis_size("lat"), lax.axis_size("lev")
    count, rows, depth, width = fields.shape
    levels = solar_profile.shape[0]
    piece = width // n_lev
    per_row = piece // BLOCK_COLS
    groups = count // LEAD
    f32 = jnp.float32
    dma = pltpu.SemaphoreType.DMA
    regular = pltpu.SemaphoreType.REGULAR
    hbm = pl.BlockSpec(memory_space=pltpu.HBM)
    vmem = pl.BlockSpec(memory_space=pltpu.VMEM)
    moved = jax.ShapeDtypeStruct((count, rows, levels, piece), f32)
    warm = jax.ShapeDtypeStruct((rows, levels, piece), f32)
    owner = jax.ShapeDtypeStruct((1, 1), f32)
    results = pl.pallas_call(
        functools.partial(kernel, n_lat, n_lev),
        out_shape=(
            pltpu.VMEM(moved.shape, f32),
            pltpu.VMEM(warm.shape, f32),
            pltpu.VMEM(owner.shape, f32),
            pltpu.VMEM((LEAD, levels, BLOCK_COLS), f32),
            pltpu.VMEM((2, levels, BLOCK_COLS), f32),
        ),
        in_specs=[hbm] * 8,
        out_specs=(vmem,) * 5,
        scratch_shapes=[
            pltpu.VMEM((count + 1, rows, depth, width), f32),
            pltpu.VMEM((rows, depth, width), f32),
            pltpu.VMEM((count, rows + 2, depth, width), f32),
            pltpu.VMEM((n_lev, rows, per_row, count, depth, BLOCK_COLS), f32),
            pltpu.VMEM((rows, per_row, count, levels, BLOCK_COLS), f32),
            pltpu.VMEM((rows, levels, piece), f32),
            pltpu.VMEM(exchange.shape, f32),
            pltpu.VMEM((1, levels), f32),
            pltpu.VMEM((rows, per_row, levels, BLOCK_COLS), f32),
            pltpu.VMEM((rows, per_row, levels, BLOCK_COLS), f32),
            pltpu.VMEM((1, BLOCK_COLS), f32),
            pltpu.VMEM((n_lat, 1, BLOCK_COLS), f32),
            pltpu.SMEM((rows * per_row,), jnp.int32),
            pltpu.SMEM((rows * per_row,), jnp.int32),
            regular,
            regular,
            dma((rows,)),
            dma,
            dma((4,)),
            dma((2,)),
            dma((2,)),
            dma,
            dma((rows,)),
            dma((rows,)),
            dma(((rows - 2 + 2 * groups) * per_row,)),
            dma,
            dma,
        ],
        compiler_params=pltpu.CompilerParams(
            collective_id=0, has_side_effects=True, vmem_limit_bytes=61400000
        ),
    )(
        fields, thickness, courant_lon, courant_lat, exchange, solar_profile[None, :],
        owners[:, 0], daylight,
    )
    return pl.pallas_call(
        store,
        out_shape=(moved, warm, owner),
        in_specs=[vmem] * 5,
        out_specs=(hbm,) * 3,
        scratch_shapes=[pltpu.VMEM((LEAD, levels, BLOCK_COLS), f32), dma((6,))],
        compiler_params=pltpu.CompilerParams(vmem_limit_bytes=12 * 1024 * 1024),
    )(*results)


def solution(mesh):
    placed = (
        P(None, "lat", "lev", None),
        P("lat", "lev", None),
        P("lat", "lev", None),
        P("lat", "lev", None),
        P(),
        P(),
        P(("lat", "lev"), None),
        P(("lat", "lev")),
    )
    return jax.shard_map(
        per_device,
        mesh=mesh,
        in_specs=placed,
        out_specs=(P(None, "lat", None, "lev"), P("lat", None, "lev"), P("lat", "lev")),
        check_vma=False,
    )
```

```python
import functools

import jax
import jax.numpy as jnp
from jax import lax
from jax.experimental import pallas as pl
from jax.experimental.pallas import tpu as pltpu
from jax.sharding import PartitionSpec as P

BLOCK_COLS = 128
THIN, THICK = 0.5, 1.5
TILE = 16
STEP = 4
LONG = 8
LEAD = 2
SPLIT = 3
HIGH = lax.Precision.HIGHEST
MESH = pl.DeviceIdType.MESH


def wendroff(values, half, half_square, plus, minus):
    return values - half * (plus - minus) + half_square * (plus - 2.0 * values + minus)


def layers_of(first, last, levels):
    def most(n):
        return levels * THICK * n / (THICK * n + THIN * (levels - n))

    def least(n):
        return levels * THIN * n / (THIN * n + THICK * (levels - n))

    slack = 0.01
    hit = [j for j in range(levels) if least(j + 1) < last + slack and most(j + 1) > first - slack]
    return hit[0] // STEP * STEP, min(levels, -(-(hit[-1] + 1) // STEP) * STEP)


def remap(levels, spacing, edges, values, count, put, slope, above):
    inverse = 1.0 / spacing
    row = lax.broadcasted_iota(jnp.int32, (TILE, BLOCK_COLS), 0)
    rise = (row + 1).astype(jnp.float32) * spacing
    top = levels - 8
    for f in range(count):
        slope[f, 0:top] = values(f, 0, top) - values(f, 1, top + 1)
        q = values(f, top, levels)
        slope[f, top:levels] = q - jnp.where(row[:8] == 7, 0.0, pltpu.roll(q, 7, 0))
    for i in range(0, levels, TILE):
        first, last = layers_of(i, i + TILE, levels)
        base = spacing * float(i)
        start, stop = first // 8 * 8, -(-last // 8) * 8
        above[start:stop] = jnp.maximum(edges(start, stop), base) - base

        def add(j0, steps, sums):
            for s in range(steps):
                j = pl.ds(j0 + s, 1)
                reach = jnp.minimum(rise, above[j, :])
                sums = tuple(total + reach * slope[f, j, :] for f, total in enumerate(sums))
            return sums

        def add_long(g, sums, add=add, first=first):
            return add(first + g * LONG, LONG, sums)

        trips, rest = divmod(last - first, LONG)
        if last < levels:
            sums = tuple(rise * values(f, last, last + 1) for f in range(count))
        else:
            sums = (jnp.zeros((TILE, BLOCK_COLS), jnp.float32),) * count
        sums = lax.fori_loop(0, trips, add_long, sums)
        if rest:
            sums = add(last - rest, rest, sums)
        for f, total in enumerate(sums):
            below = jnp.where(row == 0, 0.0, pltpu.roll(total, 1, 0))
            put(f, i, (total - below) * inverse)


def kernel(
    n_lat, n_lev,
    fields, thickness, courant_lon, courant_lat, exchange, solar, owners, daylight,
    out, heating, owner_heat, final, final_edges,
    fbuf, latbuf, stp, sbuf, rbuf, tbuf, matrix, sunbuf, upper, slope, above, shares, gathered,
    owner_of, day_of, go, lat_go,
    in_sem, lat_in_sem, small_sem, halo_send, halo_recv, thick_send, thick_recv,
    send_sem, recv_sem, share_send, share_recv,
):
    count, rows, depth, width = fields.shape
    levels = out.shape[2]
    piece = width // n_lev
    per_row = piece // BLOCK_COLS
    groups = count // LEAD
    whole = rows - SPLIT
    tail = SPLIT * per_row
    lat = lax.axis_index("lat")
    lev = lax.axis_index("lev")
    odd = lax.rem(lev, 2) == 1
    even = jnp.logical_not(odd)
    partner = lev + 1 - 2 * lax.rem(lev, 2)

    barrier = pltpu.get_barrier_semaphore()
    for d in range(1, n_lev):
        peer = lax.rem(lev + d, n_lev)

        @pl.when(lax.rem(peer, 2) == 0)
        def _():
            pl.semaphore_signal(barrier, inc=1, device_id={"lev": peer}, device_id_type=MESH)

    def load(r):
        return (
            pltpu.make_async_copy(fields.at[:, r], fbuf.at[pl.ds(0, count), r], in_sem.at[r]),
            pltpu.make_async_copy(courant_lon.at[r], fbuf.at[count, r], in_sem.at[r]),
        )

    for k in range(rows):
        for copy in load((k + rows - 1) % rows):
            copy.start()
    lat_load = pltpu.make_async_copy(courant_lat, latbuf, lat_in_sem)
    lat_load.start()
    small = ((exchange, matrix), (solar, sunbuf), (owners, owner_of), (daylight, day_of))
    small_loads = [
        pltpu.make_async_copy(source, target, small_sem.at[k])
        for k, (source, target) in enumerate(small)
    ]
    for copy in small_loads:
        copy.start()

    def span(index, size):
        return pl.ds(pl.multiple_of(index * size, size), size)

    def landed(buffer, sem):
        pltpu.make_async_copy(buffer, buffer, sem).wait()

    @pl.loop(0, rows)
    def _(r):
        pltpu.make_async_copy(
            thickness.at[r, :, span(lev, piece)], tbuf.at[r, span(lev, depth)], thick_recv.at[r]
        ).start()

    @pl.when(even)
    def _():
        pl.semaphore_wait(barrier, n_lev - 1)
        pl.semaphore_signal(go, inc=1, device_id={"lev": partner}, device_id_type=MESH)

    @pl.when(odd)
    def _():
        pl.semaphore_wait(go, 1)

        @pl.loop(1, n_lat)
        def _(d):
            pl.semaphore_signal(
                barrier, inc=1, device_id={"lat": lax.rem(lat + d, n_lat)}, device_id_type=MESH
            )

    def wait_for_lat():
        @pl.when(odd)
        def _():
            pl.semaphore_wait(barrier, n_lat - 1)
            pl.semaphore_signal(lat_go, inc=1, device_id={"lev": partner}, device_id_type=MESH)

        @pl.when(even)
        def _():
            pl.semaphore_wait(lat_go, 1)

    def thick_copy(r, d):
        target = lax.rem(lev + d, n_lev)
        return pltpu.make_async_remote_copy(
            src_ref=thickness.at[r, :, span(target, piece)],
            dst_ref=tbuf.at[r, span(lev, depth)],
            send_sem=thick_send,
            recv_sem=thick_recv.at[r],
            device_id={"lev": target},
            device_id_type=MESH,
        )

    @pl.loop(1, rows + 1)
    def _(k):
        for d in range(1, n_lev):
            thick_copy(lax.rem(k, rows), d).start()

    def lon_row(r):
        landed(fbuf.at[:, r], in_sem.at[r])

        @pl.loop(0, depth // 8)
        def _(g):
            part = span(g, 8)
            c = fbuf[count, r, part, :]
            half, half_square = 0.5 * c, 0.5 * c * c
            for f in range(count):
                q = fbuf[f, r, part, :]
                plus = pltpu.roll(q, width - 1, 1)
                minus = pltpu.roll(q, 1, 1)
                stp[f, r + 1, part, :] = wendroff(q, half, half_square, plus, minus)

    def halo(way):
        source, target = (rows, 0) if way == 0 else (1, rows + 1)
        return pltpu.make_async_remote_copy(
            src_ref=stp.at[:, source],
            dst_ref=stp.at[:, target],
            send_sem=halo_send.at[way],
            recv_sem=halo_recv.at[way],
            device_id={"lat": lax.rem(lat + (1 if way == 0 else n_lat - 1), n_lat)},
            device_id_type=MESH,
        )

    has_next = lat < n_lat - 1
    has_last = lat > 0

    @pl.loop(0, rows)
    def _(k):
        lon_row(lax.rem(k + rows - 1, rows))

    lat_load.wait()

    def picked(group):
        return pl.ds(0, count) if group is None else span(group, LEAD)

    def slot(r, b, group):
        if group is None:
            return (r - 1) * per_row + b
        return whole * per_row + group * tail + lax.rem(r + SPLIT - 1, rows) * per_row + b

    def piece_copy(r, b, d, group):
        target = lax.rem(lev + d, n_lev)
        return pltpu.make_async_remote_copy(
            src_ref=sbuf.at[target, r, b, picked(group)],
            dst_ref=rbuf.at[r, b, picked(group), span(lev, depth)],
            send_sem=send_sem.at[r],
            recv_sem=recv_sem.at[slot(r, b, group)],
            device_id={"lev": target},
            device_id_type=MESH,
        )

    def wait_piece(r, b, group=None):
        landed(rbuf.at[r, b, picked(group)], recv_sem.at[slot(r, b, group)])

    def lat_row(r):
        @pl.loop(0, depth // 8)
        def _(g):
            part = span(g, 8)
            c = latbuf[r, part, :]
            half, half_square = 0.5 * c, 0.5 * c * c
            for f in range(count):
                moved = wendroff(
                    stp[f, r + 1, part, :], half, half_square,
                    stp[f, r + 2, part, :], stp[f, r, part, :],
                )
                for p in range(n_lev):
                    for b in range(per_row):
                        at = p * piece + b * BLOCK_COLS
                        sbuf[p, r, b, f, part, :] = moved[:, at:at + BLOCK_COLS]

    def send_row(r, group=None):
        for b in range(per_row):
            for d in range(1, n_lev):
                piece_copy(r, b, d, group).start()
        for b in range(per_row):
            pltpu.make_async_copy(
                sbuf.at[lev, r, b, picked(group)],
                rbuf.at[r, b, picked(group), span(lev, depth)],
                recv_sem.at[slot(r, b, group)],
            ).start()

    @pl.loop(1, whole + 1)
    def _(r):
        lat_row(r)
        send_row(r)

    for r in range(whole + 1, rows - 1):
        lat_row(r)
        send_row(r, 0)

    wait_for_lat()

    @pl.when(has_next)
    def _():
        halo(0).start()

    @pl.when(has_last)
    def _():
        halo(1).start()

    @pl.when(jnp.logical_not(has_last))
    def _():
        stp[:, 0] = jnp.zeros((count, depth, width), jnp.float32)

    @pl.when(jnp.logical_not(has_next))
    def _():
        stp[:, rows + 1] = jnp.zeros((count, depth, width), jnp.float32)

    for copy in small_loads:
        copy.wait()
    line = lax.broadcasted_iota(jnp.int32, (levels, levels), 0)
    column = lax.broadcasted_iota(jnp.int32, (levels, levels), 1)
    sun = jnp.sum(
        jnp.where(line == column, jnp.broadcast_to(sunbuf[...], (levels, levels)), 0.0),
        axis=1, keepdims=True,
    )
    triangle = (line >= column).astype(jnp.float32)
    lanes = lax.broadcasted_iota(jnp.int32, (1, BLOCK_COLS), 1)
    shares[...] = jnp.zeros_like(shares)

    @pl.loop(1, rows + 1)
    def _(k):
        r = lax.rem(k, rows)
        landed(tbuf.at[r], thick_recv.at[r])
        edge = jnp.dot(triangle, tbuf[r], precision=HIGH, preferred_element_type=jnp.float32)
        for b in range(per_row):
            cols = slice(b * BLOCK_COLS, (b + 1) * BLOCK_COLS)
            upper[r, b] = edge[:, cols]

    def spacing_of(r, b):
        return upper[r, b, levels - 1:levels, :] / levels

    def remap_block(r, b, base, some):
        cols = span(b, BLOCK_COLS)

        def put(f, i, tile):
            out[base + f, r, i:i + TILE, cols] = tile

        remap(
            levels, spacing_of(r, b), lambda j, k: upper[r, b, j:k, :],
            lambda f, j, k: rbuf[r, b, base + f, j:k, :], some, put, slope, above,
        )

    def heat_block(r, b):
        cols = span(b, BLOCK_COLS)
        temp, humid = out[0, r, :, cols], out[1, r, :, cols]
        square = humid * humid
        clear = 1.0 / (1.0 + square)
        heat = jnp.dot(
            jnp.concatenate([matrix[k] for k in range(matrix.shape[0])], axis=1),
            jnp.concatenate([square * clear * temp, clear * temp], axis=0),
            precision=HIGH, preferred_element_type=jnp.float32,
        )
        block = r * per_row + b
        warm = heat + day_of[block].astype(jnp.float32) * sun * clear
        heating[r, :, cols] = warm
        mean = jnp.sum(jnp.sum(warm, axis=0, keepdims=True), axis=1, keepdims=True)
        mean = mean * (1.0 / (levels * BLOCK_COLS))
        shares[...] = shares[...] + jnp.where(lanes == owner_of[block], mean, 0.0)

    def share_copy(d):
        return pltpu.make_async_remote_copy(
            src_ref=shares,
            dst_ref=gathered.at[d],
            send_sem=share_send,
            recv_sem=share_recv,
            device_id={"lat": lax.rem(lat + d, n_lat)},
            device_id_type=MESH,
        )

    @pl.loop(0, whole * per_row)
    def _(c):
        b = lax.rem(c, per_row)
        r = c // per_row + 1

        @pl.when(c == min(3, whole - 1) * per_row)
        def _():
            @pl.when(has_last)
            def _():
                halo(0).wait_recv()

            @pl.when(has_next)
            def _():
                halo(1).wait_recv()

            lat_row(rows - 1)
            send_row(rows - 1, 0)
            lat_row(0)
            send_row(0, 0)
            for group in range(1, groups):
                for k in range(SPLIT):
                    send_row((whole + 1 + k) % rows, group)

        wait_piece(r, b)
        remap_block(r, b, 0, count)
        heat_block(r, b)

    def tail_block(t):
        at = lax.rem(t, tail)
        return lax.rem(whole + 1 + at // per_row, rows), lax.rem(at, per_row), t // tail

    @pl.loop(0, groups * tail - 1)
    def _(t):
        r, b, group = tail_block(t)

        wait_piece(r, b, group)
        remap_block(r, b, group * LEAD, LEAD)

        @pl.when(group == 0)
        def _():
            heat_block(r, b)

        @pl.when(t == tail - 1)
        def _():
            @pl.loop(1, n_lat)
            def _(d):
                share_copy(d).start()

    end = per_row - 1
    final_edges[...] = upper[0, end]

    landed(tbuf.at[:, pl.ds(0, depth * (n_lev - 1))], thick_send)

    @pl.when(has_next)
    def _():
        halo(0).wait_send()

    @pl.when(has_last)
    def _():
        halo(1).wait_send()

    others = gathered.at[pl.ds(1, n_lat - 1)]
    landed(others, share_recv)
    total = lax.fori_loop(1, n_lat, lambda d, total: total + gathered[d], shares[...])
    owner_heat[...] = jnp.sum(
        jnp.where(lanes == lat, total, 0.0), axis=1, keepdims=True
    )
    landed(others, share_send)

    @pl.loop(0, rows)
    def _(r):
        landed(sbuf.at[pl.ds(0, n_lev - 1), r], send_sem.at[r])

    wait_piece(0, end, groups - 1)
    final[...] = rbuf[0, end, (groups - 1) * LEAD:groups * LEAD]


def store(
    moved, warm, owner, final, edges, out, heating, owner_heat, tile, slope, above, sems,
):
    count, rows, levels, piece = moved.shape
    rest = piece - BLOCK_COLS
    kept = count - LEAD
    inner = pl.ds(1, rows - 1)
    pairs = [
        (moved.at[:, inner], out.at[:, inner]),
        (warm, heating),
        (owner, owner_heat),
        (moved.at[pl.ds(0, kept), 0], out.at[pl.ds(0, kept), 0]),
    ]
    if rest:
        pairs.append((
            moved.at[pl.ds(kept, LEAD), 0, :, pl.ds(0, rest)],
            out.at[pl.ds(kept, LEAD), 0, :, pl.ds(0, rest)],
        ))
    copies = [
        pltpu.make_async_copy(source, target, sems.at[k])
        for k, (source, target) in enumerate(pairs)
    ]
    for copy in copies:
        copy.start()

    def put(f, i, value):
        tile[f, i:i + TILE, :] = value

    remap(
        levels, edges[levels - 1:levels, :] / levels, lambda j, k: edges[j:k, :],
        lambda f, j, k: final[f, j:k, :], LEAD, put, slope, above,
    )
    last = pltpu.make_async_copy(
        tile, out.at[pl.ds(kept, LEAD), 0, :, pl.ds(rest, BLOCK_COLS)], sems.at[len(pairs)]
    )
    last.start()
    for copy in copies:
        copy.wait()
    last.wait()


def per_device(
    fields, thickness, courant_lon, courant_lat, exchange, solar_profile, owners, daylight
):
    n_lat, n_lev = lax.axis_size("lat"), lax.axis_size("lev")
    count, rows, depth, width = fields.shape
    levels = solar_profile.shape[0]
    piece = width // n_lev
    per_row = piece // BLOCK_COLS
    groups = count // LEAD
    f32 = jnp.float32
    dma = pltpu.SemaphoreType.DMA
    regular = pltpu.SemaphoreType.REGULAR
    hbm = pl.BlockSpec(memory_space=pltpu.HBM)
    vmem = pl.BlockSpec(memory_space=pltpu.VMEM)
    moved = jax.ShapeDtypeStruct((count, rows, levels, piece), f32)
    warm = jax.ShapeDtypeStruct((rows, levels, piece), f32)
    owner = jax.ShapeDtypeStruct((1, 1), f32)
    results = pl.pallas_call(
        functools.partial(kernel, n_lat, n_lev),
        out_shape=(
            pltpu.VMEM(moved.shape, f32),
            pltpu.VMEM(warm.shape, f32),
            pltpu.VMEM(owner.shape, f32),
            pltpu.VMEM((LEAD, levels, BLOCK_COLS), f32),
            pltpu.VMEM((levels, BLOCK_COLS), f32),
        ),
        in_specs=[hbm] * 8,
        out_specs=(vmem,) * 5,
        scratch_shapes=[
            pltpu.VMEM((count + 1, rows, depth, width), f32),
            pltpu.VMEM((rows, depth, width), f32),
            pltpu.VMEM((count, rows + 2, depth, width), f32),
            pltpu.VMEM((n_lev, rows, per_row, count, depth, BLOCK_COLS), f32),
            pltpu.VMEM((rows, per_row, count, levels, BLOCK_COLS), f32),
            pltpu.VMEM((rows, levels, piece), f32),
            pltpu.VMEM(exchange.shape, f32),
            pltpu.VMEM((1, levels), f32),
            pltpu.VMEM((rows, per_row, levels, BLOCK_COLS), f32),
            pltpu.VMEM((count, levels, BLOCK_COLS), f32),
            pltpu.VMEM((levels, BLOCK_COLS), f32),
            pltpu.VMEM((1, BLOCK_COLS), f32),
            pltpu.VMEM((n_lat, 1, BLOCK_COLS), f32),
            pltpu.SMEM((rows * per_row,), jnp.int32),
            pltpu.SMEM((rows * per_row,), jnp.int32),
            regular,
            regular,
            dma((rows,)),
            dma,
            dma((4,)),
            dma((2,)),
            dma((2,)),
            dma,
            dma((rows,)),
            dma((rows,)),
            dma(((rows - SPLIT + SPLIT * groups) * per_row,)),
            dma,
            dma,
        ],
        compiler_params=pltpu.CompilerParams(
            collective_id=0, has_side_effects=True, vmem_limit_bytes=61400000
        ),
    )(
        fields, thickness, courant_lon, courant_lat, exchange, solar_profile[None, :],
        owners[:, 0], daylight,
    )
    return pl.pallas_call(
        store,
        out_shape=(moved, warm, owner),
        in_specs=[vmem] * 5,
        out_specs=(hbm,) * 3,
        scratch_shapes=[
            pltpu.VMEM((LEAD, levels, BLOCK_COLS), f32),
            pltpu.VMEM((LEAD, levels, BLOCK_COLS), f32),
            pltpu.VMEM((levels, BLOCK_COLS), f32),
            dma((6,)),
        ],
        compiler_params=pltpu.CompilerParams(vmem_limit_bytes=12 * 1024 * 1024),
    )(*results)


def solution(mesh):
    placed = (
        P(None, "lat", "lev", None),
        P("lat", "lev", None),
        P("lat", "lev", None),
        P("lat", "lev", None),
        P(),
        P(),
        P(("lat", "lev"), None),
        P(("lat", "lev")),
    )
    return jax.shard_map(
        per_device,
        mesh=mesh,
        in_specs=placed,
        out_specs=(P(None, "lat", None, "lev"), P("lat", None, "lev"), P("lat", "lev")),
        check_vma=False,
    )
```

```python
import functools

import jax
import jax.numpy as jnp
from jax import lax
from jax.experimental import pallas as pl
from jax.experimental.pallas import tpu as pltpu
from jax.sharding import PartitionSpec as P

BLOCK_COLS = 128
THIN, THICK = 0.5, 1.5
TILE = 16
STEP = 4
LONG = 8
LEAD = 2
SPLIT = 3
HIGH = lax.Precision.HIGHEST
MESH = pl.DeviceIdType.MESH


def wendroff(values, half, half_square, plus, minus):
    return values - half * (plus - minus) + half_square * (plus - 2.0 * values + minus)


def layers_of(first, last, levels):
    def most(n):
        return levels * THICK * n / (THICK * n + THIN * (levels - n))

    def least(n):
        return levels * THIN * n / (THIN * n + THICK * (levels - n))

    slack = 0.01
    hit = [j for j in range(levels) if least(j + 1) < last + slack and most(j + 1) > first - slack]
    return hit[0] // STEP * STEP, min(levels, -(-(hit[-1] + 1) // STEP) * STEP)


def remap(levels, spacing, edges, values, count, put, slope, above):
    inverse = 1.0 / spacing
    row = lax.broadcasted_iota(jnp.int32, (TILE, BLOCK_COLS), 0)
    rise = (row + 1).astype(jnp.float32) * spacing
    top = levels - 8
    for f in range(count):
        slope[f, 0:top] = values(f, 0, top) - values(f, 1, top + 1)
        q = values(f, top, levels)
        slope[f, top:levels] = q - jnp.where(row[:8] == 7, 0.0, pltpu.roll(q, 7, 0))
    for i in range(0, levels, TILE):
        first, last = layers_of(i, i + TILE, levels)
        base = spacing * float(i)
        start, stop = first // 8 * 8, -(-last // 8) * 8
        above[start:stop] = jnp.maximum(edges(start, stop), base) - base

        def add(j0, steps, sums):
            for s in range(steps):
                j = pl.ds(j0 + s, 1)
                reach = jnp.minimum(rise, above[j, :])
                sums = tuple(total + reach * slope[f, j, :] for f, total in enumerate(sums))
            return sums

        def add_long(g, sums, add=add, first=first):
            return add(first + g * LONG, LONG, sums)

        trips, rest = divmod(last - first, LONG)
        if last < levels:
            sums = tuple(rise * values(f, last, last + 1) for f in range(count))
        else:
            sums = (jnp.zeros((TILE, BLOCK_COLS), jnp.float32),) * count
        sums = lax.fori_loop(0, trips, add_long, sums)
        if rest:
            sums = add(last - rest, rest, sums)
        for f, total in enumerate(sums):
            below = jnp.where(row == 0, 0.0, pltpu.roll(total, 1, 0))
            put(f, i, (total - below) * inverse)


def kernel(
    n_lat, n_lev,
    fields, thickness, courant_lon, courant_lat, exchange, solar, owners, daylight,
    out, heating, final, carried,
    fbuf, latbuf, stp, sbuf, rbuf, tbuf, matrix, sunbuf, upper, slope, above, shares, gathered,
    owner_of, day_of, go, lat_go,
    in_sem, lat_in_sem, small_sem, halo_send, halo_recv, thick_send, thick_recv,
    send_sem, recv_sem, share_send, share_recv,
):
    count, rows, depth, width = fields.shape
    levels = out.shape[2]
    piece = width // n_lev
    per_row = piece // BLOCK_COLS
    groups = count // LEAD
    whole = rows - SPLIT
    tail = SPLIT * per_row
    lat = lax.axis_index("lat")
    lev = lax.axis_index("lev")
    odd = lax.rem(lev, 2) == 1
    even = jnp.logical_not(odd)
    partner = lev + 1 - 2 * lax.rem(lev, 2)

    barrier = pltpu.get_barrier_semaphore()
    for d in range(1, n_lev):
        peer = lax.rem(lev + d, n_lev)

        @pl.when(lax.rem(peer, 2) == 0)
        def _():
            pl.semaphore_signal(barrier, inc=1, device_id={"lev": peer}, device_id_type=MESH)

    def span(index, size):
        return pl.ds(pl.multiple_of(index * size, size), size)

    def landed(buffer, sem):
        pltpu.make_async_copy(buffer, buffer, sem).wait()

    @pl.when(even)
    def _():
        pl.semaphore_wait(barrier, n_lev - 1)
        pl.semaphore_signal(go, inc=1, device_id={"lev": partner}, device_id_type=MESH)

    @pl.when(odd)
    def _():
        pl.semaphore_wait(go, 1)

    def wait_for_lat():
        @pl.when(odd)
        def _():
            pl.semaphore_wait(barrier, n_lat - 1)
            pl.semaphore_signal(lat_go, inc=1, device_id={"lev": partner}, device_id_type=MESH)

        @pl.when(even)
        def _():
            pl.semaphore_wait(lat_go, 1)

    for d in range(1, n_lev):
        target = lax.rem(lev + d, n_lev)
        pltpu.make_async_remote_copy(
            src_ref=thickness.at[:, :, span(target, piece)],
            dst_ref=tbuf.at[:, span(lev, depth)],
            send_sem=thick_send,
            recv_sem=thick_recv,
            device_id={"lev": target},
            device_id_type=MESH,
        ).start()
    pltpu.make_async_copy(fields, fbuf.at[pl.ds(0, count)], in_sem).start()
    pltpu.make_async_copy(courant_lon, fbuf.at[count], in_sem).start()
    lat_load = pltpu.make_async_copy(courant_lat, latbuf, lat_in_sem)
    lat_load.start()
    pltpu.make_async_copy(
        thickness.at[:, :, span(lev, piece)], tbuf.at[:, span(lev, depth)], thick_recv
    ).start()

    @pl.when(odd)
    def _():
        @pl.loop(1, n_lat)
        def _(d):
            pl.semaphore_signal(
                barrier, inc=1, device_id={"lat": lax.rem(lat + d, n_lat)}, device_id_type=MESH
            )

    small = ((exchange, matrix), (solar, sunbuf), (owners, owner_of), (daylight, day_of))
    small_loads = [
        pltpu.make_async_copy(source, target, small_sem.at[k])
        for k, (source, target) in enumerate(small)
    ]
    for copy in small_loads:
        copy.start()

    def lon_row(r):
        @pl.loop(0, depth // 8)
        def _(g):
            part = span(g, 8)
            c = fbuf[count, r, part, :]
            half, half_square = 0.5 * c, 0.5 * c * c
            for f in range(count):
                q = fbuf[f, r, part, :]
                plus = pltpu.roll(q, width - 1, 1)
                minus = pltpu.roll(q, 1, 1)
                stp[f, r + 1, part, :] = wendroff(q, half, half_square, plus, minus)

    def halo(way):
        source, target = (rows, 0) if way == 0 else (1, rows + 1)
        return pltpu.make_async_remote_copy(
            src_ref=stp.at[:, source],
            dst_ref=stp.at[:, target],
            send_sem=halo_send.at[way],
            recv_sem=halo_recv.at[way],
            device_id={"lat": lax.rem(lat + (1 if way == 0 else n_lat - 1), n_lat)},
            device_id_type=MESH,
        )

    has_next = lat < n_lat - 1
    has_last = lat > 0

    landed(fbuf, in_sem)

    @pl.loop(0, rows)
    def _(r):
        lon_row(r)

    lat_load.wait()

    def picked(group):
        return pl.ds(0, count) if group is None else span(group, LEAD)

    def slot(r, b, group):
        if group is None:
            return (r - 1) * per_row + b
        return whole * per_row + group * tail + lax.rem(r + SPLIT - 1, rows) * per_row + b

    def piece_copy(r, b, d, group):
        target = lax.rem(lev + d, n_lev)
        return pltpu.make_async_remote_copy(
            src_ref=sbuf.at[target, r, b, picked(group)],
            dst_ref=rbuf.at[r, b, picked(group), span(lev, depth)],
            send_sem=send_sem,
            recv_sem=recv_sem.at[slot(r, b, group)],
            device_id={"lev": target},
            device_id_type=MESH,
        )

    def wait_piece(r, b, group=None):
        landed(rbuf.at[r, b, picked(group)], recv_sem.at[slot(r, b, group)])

    def lat_row(r):
        @pl.loop(0, depth // 8)
        def _(g):
            part = span(g, 8)
            c = latbuf[r, part, :]
            half, half_square = 0.5 * c, 0.5 * c * c
            for f in range(count):
                moved = wendroff(
                    stp[f, r + 1, part, :], half, half_square,
                    stp[f, r + 2, part, :], stp[f, r, part, :],
                )
                for p in range(n_lev):
                    for b in range(per_row):
                        at = p * piece + b * BLOCK_COLS
                        sbuf[p, r, b, f, part, :] = moved[:, at:at + BLOCK_COLS]

    def send_row(r, group=None):
        for b in range(per_row):
            for d in range(1, n_lev):
                piece_copy(r, b, d, group).start()
        for b in range(per_row):
            pltpu.make_async_copy(
                sbuf.at[lev, r, b, picked(group)],
                rbuf.at[r, b, picked(group), span(lev, depth)],
                recv_sem.at[slot(r, b, group)],
            ).start()

    @pl.loop(1, whole + 1)
    def _(r):
        lat_row(r)
        send_row(r)

    for r in range(whole + 1, rows - 1):
        lat_row(r)
        send_row(r, 0)

    wait_for_lat()

    @pl.when(has_next)
    def _():
        halo(0).start()

    @pl.when(has_last)
    def _():
        halo(1).start()

    @pl.when(jnp.logical_not(has_last))
    def _():
        stp[:, 0] = jnp.zeros((count, depth, width), jnp.float32)

    @pl.when(jnp.logical_not(has_next))
    def _():
        stp[:, rows + 1] = jnp.zeros((count, depth, width), jnp.float32)

    for copy in small_loads:
        copy.wait()
    line = lax.broadcasted_iota(jnp.int32, (levels, levels), 0)
    column = lax.broadcasted_iota(jnp.int32, (levels, levels), 1)
    sun = jnp.sum(
        jnp.where(line == column, jnp.broadcast_to(sunbuf[...], (levels, levels)), 0.0),
        axis=1, keepdims=True,
    )
    triangle = (line >= column).astype(jnp.float32)
    lanes = lax.broadcasted_iota(jnp.int32, (1, BLOCK_COLS), 1)
    shares[...] = jnp.zeros_like(shares)

    landed(tbuf, thick_recv)

    @pl.loop(0, rows)
    def _(r):
        edge = jnp.dot(triangle, tbuf[r], precision=HIGH, preferred_element_type=jnp.float32)
        for b in range(per_row):
            cols = slice(b * BLOCK_COLS, (b + 1) * BLOCK_COLS)
            upper[r, b] = edge[:, cols]

    def spacing_of(r, b):
        return upper[r, b, levels - 1:levels, :] / levels

    def remap_block(r, b, base, some):
        cols = span(b, BLOCK_COLS)

        def put(f, i, tile):
            out[base + f, r, i:i + TILE, cols] = tile

        remap(
            levels, spacing_of(r, b), lambda j, k: upper[r, b, j:k, :],
            lambda f, j, k: rbuf[r, b, base + f, j:k, :], some, put, slope, above,
        )

    def heat_block(r, b):
        cols = span(b, BLOCK_COLS)
        temp, humid = out[0, r, :, cols], out[1, r, :, cols]
        square = humid * humid
        clear = 1.0 / (1.0 + square)
        heat = jnp.dot(
            jnp.concatenate([matrix[k] for k in range(matrix.shape[0])], axis=1),
            jnp.concatenate([square * clear * temp, clear * temp], axis=0),
            precision=HIGH, preferred_element_type=jnp.float32,
        )
        block = r * per_row + b
        warm = heat + day_of[block].astype(jnp.float32) * sun * clear
        heating[r, :, cols] = warm
        mean = jnp.sum(jnp.sum(warm, axis=0, keepdims=True), axis=1, keepdims=True)
        mean = mean * (1.0 / (levels * BLOCK_COLS))
        shares[...] = shares[...] + jnp.where(lanes == owner_of[block], mean, 0.0)

    def share_copy(d):
        return pltpu.make_async_remote_copy(
            src_ref=shares,
            dst_ref=gathered.at[d],
            send_sem=share_send,
            recv_sem=share_recv,
            device_id={"lat": lax.rem(lat + d, n_lat)},
            device_id_type=MESH,
        )

    @pl.loop(0, whole * per_row)
    def _(c):
        b = lax.rem(c, per_row)
        r = c // per_row + 1

        @pl.when(c == min(3, whole - 1) * per_row)
        def _():
            @pl.when(has_last)
            def _():
                halo(0).wait_recv()

            @pl.when(has_next)
            def _():
                halo(1).wait_recv()

            lat_row(rows - 1)
            send_row(rows - 1, 0)
            lat_row(0)
            send_row(0, 0)
            for group in range(1, groups):
                for k in range(SPLIT):
                    send_row((whole + 1 + k) % rows, group)

        wait_piece(r, b)
        remap_block(r, b, 0, count)
        heat_block(r, b)

    def tail_block(t):
        at = lax.rem(t, tail)
        return lax.rem(whole + 1 + at // per_row, rows), lax.rem(at, per_row), t // tail

    @pl.loop(0, groups * tail - 1)
    def _(t):
        r, b, group = tail_block(t)

        wait_piece(r, b, group)
        remap_block(r, b, group * LEAD, LEAD)

        @pl.when(group == 0)
        def _():
            heat_block(r, b)

        @pl.when(t == tail - 1)
        def _():
            @pl.loop(1, n_lat)
            def _(d):
                share_copy(d).start()

    end = per_row - 1
    carried[0:levels] = upper[0, end]

    landed(tbuf.at[:, pl.ds(0, depth * (n_lev - 1))], thick_send)

    @pl.when(has_next)
    def _():
        halo(0).wait_send()

    @pl.when(has_last)
    def _():
        halo(1).wait_send()

    others = gathered.at[pl.ds(1, n_lat - 1)]
    landed(others, share_recv)
    total = lax.fori_loop(1, n_lat, lambda d, total: total + gathered[d], shares[...])
    own = jnp.sum(jnp.where(lanes == lat, total, 0.0), axis=1, keepdims=True)
    carried[levels:] = jnp.broadcast_to(own, (8, BLOCK_COLS))
    landed(others, share_send)

    landed(sbuf.at[pl.ds(0, n_lev - 1)], send_sem)

    wait_piece(0, end, groups - 1)
    final[...] = rbuf[0, end, (groups - 1) * LEAD:groups * LEAD]


def store(
    moved, warm, final, carried, out, heating, owner_heat, tile, slope, above, owner, sems,
):
    count, rows, levels, piece = moved.shape
    rest = piece - BLOCK_COLS
    kept = count - LEAD
    owner[...] = carried[levels:levels + 1, 0:1]
    inner = pl.ds(1, rows - 1)
    pairs = [
        (moved.at[:, inner], out.at[:, inner]),
        (warm, heating),
        (owner, owner_heat),
        (moved.at[pl.ds(0, kept), 0], out.at[pl.ds(0, kept), 0]),
    ]
    if rest:
        pairs.append((
            moved.at[pl.ds(kept, LEAD), 0, :, pl.ds(0, rest)],
            out.at[pl.ds(kept, LEAD), 0, :, pl.ds(0, rest)],
        ))
    copies = [
        pltpu.make_async_copy(source, target, sems.at[k])
        for k, (source, target) in enumerate(pairs)
    ]
    for copy in copies:
        copy.start()

    def put(f, i, value):
        tile[f, i:i + TILE, :] = value

    remap(
        levels, carried[levels - 1:levels, :] / levels, lambda j, k: carried[j:k, :],
        lambda f, j, k: final[f, j:k, :], LEAD, put, slope, above,
    )
    last = pltpu.make_async_copy(
        tile, out.at[pl.ds(kept, LEAD), 0, :, pl.ds(rest, BLOCK_COLS)], sems.at[len(pairs)]
    )
    last.start()
    for copy in copies:
        copy.wait()
    last.wait()


def per_device(
    fields, thickness, courant_lon, courant_lat, exchange, solar_profile, owners, daylight
):
    n_lat, n_lev = lax.axis_size("lat"), lax.axis_size("lev")
    count, rows, depth, width = fields.shape
    levels = solar_profile.shape[0]
    piece = width // n_lev
    per_row = piece // BLOCK_COLS
    groups = count // LEAD
    f32 = jnp.float32
    dma = pltpu.SemaphoreType.DMA
    regular = pltpu.SemaphoreType.REGULAR
    hbm = pl.BlockSpec(memory_space=pltpu.HBM)
    vmem = pl.BlockSpec(memory_space=pltpu.VMEM)
    moved = jax.ShapeDtypeStruct((count, rows, levels, piece), f32)
    warm = jax.ShapeDtypeStruct((rows, levels, piece), f32)
    owner = jax.ShapeDtypeStruct((1, 1), f32)
    results = pl.pallas_call(
        functools.partial(kernel, n_lat, n_lev),
        out_shape=(
            pltpu.VMEM(moved.shape, f32),
            pltpu.VMEM(warm.shape, f32),
            pltpu.VMEM((LEAD, levels, BLOCK_COLS), f32),
            pltpu.VMEM((levels + 8, BLOCK_COLS), f32),
        ),
        in_specs=[hbm] * 8,
        out_specs=(vmem,) * 4,
        scratch_shapes=[
            pltpu.VMEM((count + 1, rows, depth, width), f32),
            pltpu.VMEM((rows, depth, width), f32),
            pltpu.VMEM((count, rows + 2, depth, width), f32),
            pltpu.VMEM((n_lev, rows, per_row, count, depth, BLOCK_COLS), f32),
            pltpu.VMEM((rows, per_row, count, levels, BLOCK_COLS), f32),
            pltpu.VMEM((rows, levels, piece), f32),
            pltpu.VMEM(exchange.shape, f32),
            pltpu.VMEM((1, levels), f32),
            pltpu.VMEM((rows, per_row, levels, BLOCK_COLS), f32),
            pltpu.VMEM((count, levels, BLOCK_COLS), f32),
            pltpu.VMEM((levels, BLOCK_COLS), f32),
            pltpu.VMEM((1, BLOCK_COLS), f32),
            pltpu.VMEM((n_lat, 1, BLOCK_COLS), f32),
            pltpu.SMEM((rows * per_row,), jnp.int32),
            pltpu.SMEM((rows * per_row,), jnp.int32),
            regular,
            regular,
            dma,
            dma,
            dma((4,)),
            dma((2,)),
            dma((2,)),
            dma,
            dma,
            dma,
            dma(((rows - SPLIT + SPLIT * groups) * per_row,)),
            dma,
            dma,
        ],
        compiler_params=pltpu.CompilerParams(
            collective_id=0, has_side_effects=True, vmem_limit_bytes=61400000
        ),
    )(
        fields, thickness, courant_lon, courant_lat, exchange, solar_profile[None, :],
        owners[:, 0], daylight,
    )
    return pl.pallas_call(
        store,
        out_shape=(moved, warm, owner),
        in_specs=[vmem] * 4,
        out_specs=(hbm,) * 3,
        scratch_shapes=[
            pltpu.VMEM((LEAD, levels, BLOCK_COLS), f32),
            pltpu.VMEM((LEAD, levels, BLOCK_COLS), f32),
            pltpu.VMEM((levels, BLOCK_COLS), f32),
            pltpu.VMEM(owner.shape, f32),
            dma((6,)),
        ],
        compiler_params=pltpu.CompilerParams(vmem_limit_bytes=12 * 1024 * 1024),
    )(*results)


def solution(mesh):
    placed = (
        P(None, "lat", "lev", None),
        P("lat", "lev", None),
        P("lat", "lev", None),
        P("lat", "lev", None),
        P(),
        P(),
        P(("lat", "lev"), None),
        P(("lat", "lev")),
    )
    return jax.shard_map(
        per_device,
        mesh=mesh,
        in_specs=placed,
        out_specs=(P(None, "lat", None, "lev"), P("lat", None, "lev"), P("lat", "lev")),
        check_vma=False,
    )
```

```python
import functools

import jax
import jax.numpy as jnp
from jax import lax
from jax.experimental import pallas as pl
from jax.experimental.pallas import tpu as pltpu
from jax.sharding import PartitionSpec as P

BLOCK_COLS = 128
THIN, THICK = 0.5, 1.5
TILE = 16
STEP = 4
LONG = 8
LEAD = 2
SPLIT = 3
HIGH = lax.Precision.HIGHEST
MESH = pl.DeviceIdType.MESH


def wendroff(values, half, half_square, plus, minus):
    return values - half * (plus - minus) + half_square * (plus - 2.0 * values + minus)


def layers_of(first, last, levels):
    def most(n):
        return levels * THICK * n / (THICK * n + THIN * (levels - n))

    def least(n):
        return levels * THIN * n / (THIN * n + THICK * (levels - n))

    slack = 0.01
    hit = [j for j in range(levels) if least(j + 1) < last + slack and most(j + 1) > first - slack]
    return hit[0] // STEP * STEP, min(levels, -(-(hit[-1] + 1) // STEP) * STEP)


def remap(levels, spacing, edges, values, count, put, slope, above):
    inverse = 1.0 / spacing
    row = lax.broadcasted_iota(jnp.int32, (TILE, BLOCK_COLS), 0)
    rise = (row + 1).astype(jnp.float32) * spacing
    top = levels - 8
    for f in range(count):
        slope[f, 0:top] = values(f, 0, top) - values(f, 1, top + 1)
        q = values(f, top, levels)
        slope[f, top:levels] = q - jnp.where(row[:8] == 7, 0.0, pltpu.roll(q, 7, 0))
    for i in range(0, levels, TILE):
        first, last = layers_of(i, i + TILE, levels)
        base = spacing * float(i)
        start, stop = first // 8 * 8, -(-last // 8) * 8
        above[start:stop] = jnp.maximum(edges(start, stop), base) - base

        def add(j0, steps, sums):
            for s in range(steps):
                j = pl.ds(j0 + s, 1)
                reach = jnp.minimum(rise, above[j, :])
                sums = tuple(total + reach * slope[f, j, :] for f, total in enumerate(sums))
            return sums

        def add_long(g, sums, add=add, first=first):
            return add(first + g * LONG, LONG, sums)

        trips, rest = divmod(last - first, LONG)
        if last < levels:
            sums = tuple(rise * values(f, last, last + 1) for f in range(count))
        else:
            sums = (jnp.zeros((TILE, BLOCK_COLS), jnp.float32),) * count
        sums = lax.fori_loop(0, trips, add_long, sums)
        if rest:
            sums = add(last - rest, rest, sums)
        for f, total in enumerate(sums):
            below = jnp.where(row == 0, 0.0, pltpu.roll(total, 1, 0))
            put(f, i, (total - below) * inverse)


def kernel(
    n_lat, n_lev,
    fields, thickness, courant_lon, courant_lat, exchange, solar, owners, daylight,
    out, heating, final, carried,
    fbuf, latbuf, stp, sbuf, rbuf, tbuf, matrix, sunbuf, upper, slope, above, shares, gathered,
    owner_of, day_of, go, lat_go,
    in_sem, lat_in_sem, small_sem, halo_send, halo_recv, thick_send, thick_recv,
    send_sem, recv_sem, share_send, share_recv,
):
    count, rows, depth, width = fields.shape
    levels = out.shape[2]
    piece = width // n_lev
    per_row = piece // BLOCK_COLS
    groups = count // LEAD
    whole = rows - SPLIT
    tail = SPLIT * per_row
    lat = lax.axis_index("lat")
    lev = lax.axis_index("lev")
    odd = lax.rem(lev, 2) == 1
    even = jnp.logical_not(odd)
    partner = lev + 1 - 2 * lax.rem(lev, 2)

    barrier = pltpu.get_barrier_semaphore()
    for d in range(1, n_lev):
        peer = lax.rem(lev + d, n_lev)

        @pl.when(lax.rem(peer, 2) == 0)
        def _():
            pl.semaphore_signal(barrier, inc=1, device_id={"lev": peer}, device_id_type=MESH)

    def span(index, size):
        return pl.ds(pl.multiple_of(index * size, size), size)

    def landed(buffer, sem):
        pltpu.make_async_copy(buffer, buffer, sem).wait()

    @pl.when(even)
    def _():
        pl.semaphore_wait(barrier, n_lev - 1)
        pl.semaphore_signal(go, inc=1, device_id={"lev": partner}, device_id_type=MESH)

    @pl.when(odd)
    def _():
        pl.semaphore_wait(go, 1)

    def wait_for_lat():
        @pl.when(odd)
        def _():
            pl.semaphore_wait(barrier, n_lat - 1)
            pl.semaphore_signal(lat_go, inc=1, device_id={"lev": partner}, device_id_type=MESH)

        @pl.when(even)
        def _():
            pl.semaphore_wait(lat_go, 1)

    first = lev - lax.rem(lev, 2)
    peers = [lax.rem(first + d, n_lev) for d in range(2, n_lev)] + [partner]

    for target in peers:
        pltpu.make_async_remote_copy(
            src_ref=thickness.at[:, :, span(target, piece)],
            dst_ref=tbuf.at[:, span(lev, depth)],
            send_sem=thick_send,
            recv_sem=thick_recv,
            device_id={"lev": target},
            device_id_type=MESH,
        ).start()
    pltpu.make_async_copy(fields, fbuf.at[pl.ds(0, count)], in_sem).start()
    pltpu.make_async_copy(courant_lon, fbuf.at[count], in_sem).start()
    lat_load = pltpu.make_async_copy(courant_lat, latbuf, lat_in_sem)
    lat_load.start()
    pltpu.make_async_copy(
        thickness.at[:, :, span(lev, piece)], tbuf.at[:, span(lev, depth)], thick_recv
    ).start()

    @pl.when(odd)
    def _():
        @pl.loop(1, n_lat)
        def _(d):
            pl.semaphore_signal(
                barrier, inc=1, device_id={"lat": lax.rem(lat + d, n_lat)}, device_id_type=MESH
            )

    small = ((exchange, matrix), (solar, sunbuf), (owners, owner_of), (daylight, day_of))
    small_loads = [
        pltpu.make_async_copy(source, target, small_sem.at[k])
        for k, (source, target) in enumerate(small)
    ]
    for copy in small_loads:
        copy.start()

    def lon_row(r):
        @pl.loop(0, depth // 8)
        def _(g):
            part = span(g, 8)
            c = fbuf[count, r, part, :]
            half, half_square = 0.5 * c, 0.5 * c * c
            for f in range(count):
                q = fbuf[f, r, part, :]
                plus = pltpu.roll(q, width - 1, 1)
                minus = pltpu.roll(q, 1, 1)
                stp[f, r + 1, part, :] = wendroff(q, half, half_square, plus, minus)

    def halo(way):
        source, target = (rows, 0) if way == 0 else (1, rows + 1)
        return pltpu.make_async_remote_copy(
            src_ref=stp.at[:, source],
            dst_ref=stp.at[:, target],
            send_sem=halo_send.at[way],
            recv_sem=halo_recv.at[way],
            device_id={"lat": lax.rem(lat + (1 if way == 0 else n_lat - 1), n_lat)},
            device_id_type=MESH,
        )

    has_next = lat < n_lat - 1
    has_last = lat > 0

    landed(fbuf, in_sem)

    @pl.loop(0, rows)
    def _(r):
        lon_row(r)

    lat_load.wait()

    def picked(group):
        return pl.ds(0, count) if group is None else span(group, LEAD)

    def slot(r, b, group):
        if group is None:
            return (r - 1) * per_row + b
        return whole * per_row + group * tail + lax.rem(r + SPLIT - 1, rows) * per_row + b

    def piece_copy(r, b, target, group):
        return pltpu.make_async_remote_copy(
            src_ref=sbuf.at[target, r, b, picked(group)],
            dst_ref=rbuf.at[r, b, picked(group), span(lev, depth)],
            send_sem=send_sem,
            recv_sem=recv_sem.at[slot(r, b, group)],
            device_id={"lev": target},
            device_id_type=MESH,
        )

    def wait_piece(r, b, group=None):
        landed(rbuf.at[r, b, picked(group)], recv_sem.at[slot(r, b, group)])

    def lat_row(r):
        @pl.loop(0, depth // 8)
        def _(g):
            part = span(g, 8)
            c = latbuf[r, part, :]
            half, half_square = 0.5 * c, 0.5 * c * c
            for f in range(count):
                moved = wendroff(
                    stp[f, r + 1, part, :], half, half_square,
                    stp[f, r + 2, part, :], stp[f, r, part, :],
                )
                for p in range(n_lev):
                    for b in range(per_row):
                        at = p * piece + b * BLOCK_COLS
                        sbuf[p, r, b, f, part, :] = moved[:, at:at + BLOCK_COLS]

    def send_row(r, group=None):
        for b in range(per_row):
            for target in peers:
                piece_copy(r, b, target, group).start()
        for b in range(per_row):
            pltpu.make_async_copy(
                sbuf.at[lev, r, b, picked(group)],
                rbuf.at[r, b, picked(group), span(lev, depth)],
                recv_sem.at[slot(r, b, group)],
            ).start()

    @pl.loop(1, whole + 1)
    def _(r):
        lat_row(r)
        send_row(r)

    for r in range(whole + 1, rows - 1):
        lat_row(r)
        send_row(r, 0)

    wait_for_lat()

    @pl.when(has_next)
    def _():
        halo(0).start()

    @pl.when(has_last)
    def _():
        halo(1).start()

    @pl.when(jnp.logical_not(has_last))
    def _():
        stp[:, 0] = jnp.zeros((count, depth, width), jnp.float32)

    @pl.when(jnp.logical_not(has_next))
    def _():
        stp[:, rows + 1] = jnp.zeros((count, depth, width), jnp.float32)

    for copy in small_loads:
        copy.wait()
    line = lax.broadcasted_iota(jnp.int32, (levels, levels), 0)
    column = lax.broadcasted_iota(jnp.int32, (levels, levels), 1)
    sun = jnp.sum(
        jnp.where(line == column, jnp.broadcast_to(sunbuf[...], (levels, levels)), 0.0),
        axis=1, keepdims=True,
    )
    triangle = (line >= column).astype(jnp.float32)
    lanes = lax.broadcasted_iota(jnp.int32, (1, BLOCK_COLS), 1)
    shares[...] = jnp.zeros_like(shares)

    landed(tbuf, thick_recv)

    @pl.loop(0, rows)
    def _(r):
        edge = jnp.dot(triangle, tbuf[r], precision=HIGH, preferred_element_type=jnp.float32)
        for b in range(per_row):
            cols = slice(b * BLOCK_COLS, (b + 1) * BLOCK_COLS)
            upper[r, b] = edge[:, cols]

    def spacing_of(r, b):
        return upper[r, b, levels - 1:levels, :] / levels

    def remap_block(r, b, base, some):
        cols = span(b, BLOCK_COLS)

        def put(f, i, tile):
            out[base + f, r, i:i + TILE, cols] = tile

        remap(
            levels, spacing_of(r, b), lambda j, k: upper[r, b, j:k, :],
            lambda f, j, k: rbuf[r, b, base + f, j:k, :], some, put, slope, above,
        )

    def heat_block(r, b):
        cols = span(b, BLOCK_COLS)
        temp, humid = out[0, r, :, cols], out[1, r, :, cols]
        square = humid * humid
        clear = 1.0 / (1.0 + square)
        heat = jnp.dot(
            jnp.concatenate([matrix[k] for k in range(matrix.shape[0])], axis=1),
            jnp.concatenate([square * clear * temp, clear * temp], axis=0),
            precision=HIGH, preferred_element_type=jnp.float32,
        )
        block = r * per_row + b
        warm = heat + day_of[block].astype(jnp.float32) * sun * clear
        heating[r, :, cols] = warm
        mean = jnp.sum(jnp.sum(warm, axis=0, keepdims=True), axis=1, keepdims=True)
        mean = mean * (1.0 / (levels * BLOCK_COLS))
        shares[...] = shares[...] + jnp.where(lanes == owner_of[block], mean, 0.0)

    def share_copy(d):
        return pltpu.make_async_remote_copy(
            src_ref=shares,
            dst_ref=gathered.at[d],
            send_sem=share_send,
            recv_sem=share_recv,
            device_id={"lat": lax.rem(lat + d, n_lat)},
            device_id_type=MESH,
        )

    @pl.loop(0, whole * per_row)
    def _(c):
        b = lax.rem(c, per_row)
        r = c // per_row + 1

        @pl.when(c == min(3, whole - 1) * per_row)
        def _():
            @pl.when(has_last)
            def _():
                halo(0).wait_recv()

            @pl.when(has_next)
            def _():
                halo(1).wait_recv()

            lat_row(rows - 1)
            send_row(rows - 1, 0)
            lat_row(0)
            send_row(0, 0)
            for group in range(1, groups):
                for k in range(SPLIT):
                    send_row((whole + 1 + k) % rows, group)

        wait_piece(r, b)
        remap_block(r, b, 0, count)
        heat_block(r, b)

    def tail_block(t):
        at = lax.rem(t, tail)
        return lax.rem(whole + 1 + at // per_row, rows), lax.rem(at, per_row), t // tail

    @pl.loop(0, groups * tail - 1)
    def _(t):
        r, b, group = tail_block(t)

        wait_piece(r, b, group)
        remap_block(r, b, group * LEAD, LEAD)

        @pl.when(group == 0)
        def _():
            heat_block(r, b)

        @pl.when(t == tail - 1)
        def _():
            @pl.loop(1, n_lat)
            def _(d):
                share_copy(d).start()

    end = per_row - 1
    carried[0:levels] = upper[0, end]

    landed(tbuf.at[:, pl.ds(0, depth * (n_lev - 1))], thick_send)

    @pl.when(has_next)
    def _():
        halo(0).wait_send()

    @pl.when(has_last)
    def _():
        halo(1).wait_send()

    others = gathered.at[pl.ds(1, n_lat - 1)]
    landed(others, share_recv)
    total = lax.fori_loop(1, n_lat, lambda d, total: total + gathered[d], shares[...])
    own = jnp.sum(jnp.where(lanes == lat, total, 0.0), axis=1, keepdims=True)
    carried[levels:] = jnp.broadcast_to(own, (8, BLOCK_COLS))
    landed(others, share_send)

    landed(sbuf.at[pl.ds(0, n_lev - 1)], send_sem)

    wait_piece(0, end, groups - 1)
    final[...] = rbuf[0, end, (groups - 1) * LEAD:groups * LEAD]


def store(
    moved, warm, final, carried, out, heating, owner_heat, tile, slope, above, owner, sems,
):
    count, rows, levels, piece = moved.shape
    rest = piece - BLOCK_COLS
    kept = count - LEAD
    owner[...] = carried[levels:levels + 1, 0:1]
    inner = pl.ds(1, rows - 1)
    pairs = [
        (moved.at[:, inner], out.at[:, inner]),
        (warm, heating),
        (owner, owner_heat),
        (moved.at[pl.ds(0, kept), 0], out.at[pl.ds(0, kept), 0]),
    ]
    if rest:
        pairs.append((
            moved.at[pl.ds(kept, LEAD), 0, :, pl.ds(0, rest)],
            out.at[pl.ds(kept, LEAD), 0, :, pl.ds(0, rest)],
        ))
    copies = [
        pltpu.make_async_copy(source, target, sems.at[k])
        for k, (source, target) in enumerate(pairs)
    ]
    for copy in copies:
        copy.start()

    def put(f, i, value):
        tile[f, i:i + TILE, :] = value

    remap(
        levels, carried[levels - 1:levels, :] / levels, lambda j, k: carried[j:k, :],
        lambda f, j, k: final[f, j:k, :], LEAD, put, slope, above,
    )
    last = pltpu.make_async_copy(
        tile, out.at[pl.ds(kept, LEAD), 0, :, pl.ds(rest, BLOCK_COLS)], sems.at[len(pairs)]
    )
    last.start()
    for copy in copies:
        copy.wait()
    last.wait()


def per_device(
    fields, thickness, courant_lon, courant_lat, exchange, solar_profile, owners, daylight
):
    n_lat, n_lev = lax.axis_size("lat"), lax.axis_size("lev")
    count, rows, depth, width = fields.shape
    levels = solar_profile.shape[0]
    piece = width // n_lev
    per_row = piece // BLOCK_COLS
    groups = count // LEAD
    f32 = jnp.float32
    dma = pltpu.SemaphoreType.DMA
    regular = pltpu.SemaphoreType.REGULAR
    hbm = pl.BlockSpec(memory_space=pltpu.HBM)
    vmem = pl.BlockSpec(memory_space=pltpu.VMEM)
    moved = jax.ShapeDtypeStruct((count, rows, levels, piece), f32)
    warm = jax.ShapeDtypeStruct((rows, levels, piece), f32)
    owner = jax.ShapeDtypeStruct((1, 1), f32)
    results = pl.pallas_call(
        functools.partial(kernel, n_lat, n_lev),
        out_shape=(
            pltpu.VMEM(moved.shape, f32),
            pltpu.VMEM(warm.shape, f32),
            pltpu.VMEM((LEAD, levels, BLOCK_COLS), f32),
            pltpu.VMEM((levels + 8, BLOCK_COLS), f32),
        ),
        in_specs=[hbm] * 8,
        out_specs=(vmem,) * 4,
        scratch_shapes=[
            pltpu.VMEM((count + 1, rows, depth, width), f32),
            pltpu.VMEM((rows, depth, width), f32),
            pltpu.VMEM((count, rows + 2, depth, width), f32),
            pltpu.VMEM((n_lev, rows, per_row, count, depth, BLOCK_COLS), f32),
            pltpu.VMEM((rows, per_row, count, levels, BLOCK_COLS), f32),
            pltpu.VMEM((rows, levels, piece), f32),
            pltpu.VMEM(exchange.shape, f32),
            pltpu.VMEM((1, levels), f32),
            pltpu.VMEM((rows, per_row, levels, BLOCK_COLS), f32),
            pltpu.VMEM((count, levels, BLOCK_COLS), f32),
            pltpu.VMEM((levels, BLOCK_COLS), f32),
            pltpu.VMEM((1, BLOCK_COLS), f32),
            pltpu.VMEM((n_lat, 1, BLOCK_COLS), f32),
            pltpu.SMEM((rows * per_row,), jnp.int32),
            pltpu.SMEM((rows * per_row,), jnp.int32),
            regular,
            regular,
            dma,
            dma,
            dma((4,)),
            dma((2,)),
            dma((2,)),
            dma,
            dma,
            dma,
            dma(((rows - SPLIT + SPLIT * groups) * per_row,)),
            dma,
            dma,
        ],
        compiler_params=pltpu.CompilerParams(
            collective_id=0, has_side_effects=True, vmem_limit_bytes=61400000
        ),
    )(
        fields, thickness, courant_lon, courant_lat, exchange, solar_profile[None, :],
        owners[:, 0], daylight,
    )
    return pl.pallas_call(
        store,
        out_shape=(moved, warm, owner),
        in_specs=[vmem] * 4,
        out_specs=(hbm,) * 3,
        scratch_shapes=[
            pltpu.VMEM((LEAD, levels, BLOCK_COLS), f32),
            pltpu.VMEM((LEAD, levels, BLOCK_COLS), f32),
            pltpu.VMEM((levels, BLOCK_COLS), f32),
            pltpu.VMEM(owner.shape, f32),
            dma((6,)),
        ],
        compiler_params=pltpu.CompilerParams(vmem_limit_bytes=12 * 1024 * 1024),
    )(*results)


def solution(mesh):
    placed = (
        P(None, "lat", "lev", None),
        P("lat", "lev", None),
        P("lat", "lev", None),
        P("lat", "lev", None),
        P(),
        P(),
        P(("lat", "lev"), None),
        P(("lat", "lev")),
    )
    return jax.shard_map(
        per_device,
        mesh=mesh,
        in_specs=placed,
        out_specs=(P(None, "lat", None, "lev"), P("lat", None, "lev"), P("lat", "lev")),
        check_vma=False,
    )
```

```python
import functools

import jax
import jax.numpy as jnp
from jax import lax
from jax.experimental import pallas as pl
from jax.experimental.pallas import tpu as pltpu
from jax.sharding import PartitionSpec as P

BLOCK_COLS = 128
THIN, THICK = 0.5, 1.5
TILE = 16
STEP = 4
LONG = 8
LEAD = 2
SPLIT = 3
HIGH = lax.Precision.HIGHEST
MESH = pl.DeviceIdType.MESH


def wendroff(values, half, half_square, plus, minus):
    return values - half * (plus - minus) + half_square * (plus - 2.0 * values + minus)


def layers_of(first, last, levels):
    def most(n):
        return levels * THICK * n / (THICK * n + THIN * (levels - n))

    def least(n):
        return levels * THIN * n / (THIN * n + THICK * (levels - n))

    slack = 0.01
    hit = [j for j in range(levels) if least(j + 1) < last + slack and most(j + 1) > first - slack]
    return hit[0] // STEP * STEP, min(levels, -(-(hit[-1] + 1) // STEP) * STEP)


def remap(levels, spacing, edges, values, count, put, slope, above):
    inverse = 1.0 / spacing
    row = lax.broadcasted_iota(jnp.int32, (TILE, BLOCK_COLS), 0)
    rise = (row + 1).astype(jnp.float32) * spacing
    top = levels - 8
    for f in range(count):
        slope[f, 0:top] = values(f, 0, top) - values(f, 1, top + 1)
        q = values(f, top, levels)
        slope[f, top:levels] = q - jnp.where(row[:8] == 7, 0.0, pltpu.roll(q, 7, 0))
    for i in range(0, levels, TILE):
        first, last = layers_of(i, i + TILE, levels)
        base = spacing * float(i)
        start, stop = first // 8 * 8, -(-last // 8) * 8
        above[start:stop] = jnp.maximum(edges(start, stop), base) - base

        def add(j0, steps, sums):
            for s in range(steps):
                j = pl.ds(j0 + s, 1)
                reach = jnp.minimum(rise, above[j, :])
                sums = tuple(total + reach * slope[f, j, :] for f, total in enumerate(sums))
            return sums

        def add_long(g, sums, add=add, first=first):
            return add(first + g * LONG, LONG, sums)

        trips, rest = divmod(last - first, LONG)
        if last < levels:
            sums = tuple(rise * values(f, last, last + 1) for f in range(count))
        else:
            sums = (jnp.zeros((TILE, BLOCK_COLS), jnp.float32),) * count
        sums = lax.fori_loop(0, trips, add_long, sums)
        if rest:
            sums = add(last - rest, rest, sums)
        for f, total in enumerate(sums):
            below = jnp.where(row == 0, 0.0, pltpu.roll(total, 1, 0))
            put(f, i, (total - below) * inverse)


def kernel(
    n_lat, n_lev,
    fields, thickness, courant_lon, courant_lat, exchange, solar, owners, daylight,
    out, heating, final, carried,
    fbuf, stp, sbuf, rbuf, tbuf, matrix, sunbuf, upper, slope, above, shares, gathered,
    owner_of, day_of, word,
    in_sem, small_sem, halo_send, halo_recv, thick_send, thick_recv,
    send_sem, recv_sem, share_send, share_recv,
):
    count, rows, depth, width = fields.shape
    levels = out.shape[2]
    piece = width // n_lev
    per_row = piece // BLOCK_COLS
    groups = count // LEAD
    whole = rows - SPLIT
    tail = SPLIT * per_row
    lat = lax.axis_index("lat")
    lev = lax.axis_index("lev")
    odd = lax.rem(lev, 2) == 1
    even = jnp.logical_not(odd)
    partner = lev + 1 - 2 * lax.rem(lev, 2)

    barrier = pltpu.get_barrier_semaphore()
    for d in range(1, n_lev):
        peer = lax.rem(lev + d, n_lev)

        @pl.when(lax.rem(peer, 2) == 0)
        def _():
            pl.semaphore_signal(barrier, inc=1, device_id={"lev": peer}, device_id_type=MESH)

    def span(index, size):
        return pl.ds(pl.multiple_of(index * size, size), size)

    def landed(buffer, sem):
        pltpu.make_async_copy(buffer, buffer, sem).wait()

    @pl.when(even)
    def _():
        pl.semaphore_wait(barrier, n_lev - 1)
        pl.semaphore_signal(word, inc=1, device_id={"lev": partner}, device_id_type=MESH)

    @pl.when(odd)
    def _():
        pl.semaphore_wait(word, 1)

    def wait_for_lat():
        @pl.when(odd)
        def _():
            pl.semaphore_wait(barrier, n_lat - 1)
            pl.semaphore_signal(word, inc=1, device_id={"lev": partner}, device_id_type=MESH)

        @pl.when(even)
        def _():
            pl.semaphore_wait(word, 1)

    first = lev - lax.rem(lev, 2)
    peers = [lax.rem(first + d, n_lev) for d in range(2, n_lev)] + [partner]

    for target in peers:
        pltpu.make_async_remote_copy(
            src_ref=thickness.at[:, :, span(target, piece)],
            dst_ref=tbuf.at[:, span(lev, depth)],
            send_sem=thick_send,
            recv_sem=thick_recv,
            device_id={"lev": target},
            device_id_type=MESH,
        ).start()
    pltpu.make_async_copy(fields, fbuf.at[pl.ds(0, count)], in_sem).start()
    pltpu.make_async_copy(courant_lon, fbuf.at[count], in_sem).start()
    pltpu.make_async_copy(courant_lat, fbuf.at[count + 1], in_sem).start()
    pltpu.make_async_copy(
        thickness.at[:, :, span(lev, piece)], tbuf.at[:, span(lev, depth)], thick_recv
    ).start()

    @pl.when(odd)
    def _():
        @pl.loop(1, n_lat)
        def _(d):
            pl.semaphore_signal(
                barrier, inc=1, device_id={"lat": lax.rem(lat + d, n_lat)}, device_id_type=MESH
            )

    small = ((exchange, matrix), (solar, sunbuf), (owners, owner_of), (daylight, day_of))
    small_loads = [
        pltpu.make_async_copy(source, target, small_sem.at[k])
        for k, (source, target) in enumerate(small)
    ]
    for copy in small_loads:
        copy.start()

    def lon_row(r):
        @pl.loop(0, depth // 8)
        def _(g):
            part = span(g, 8)
            c = fbuf[count, r, part, :]
            half, half_square = 0.5 * c, 0.5 * c * c
            for f in range(count):
                q = fbuf[f, r, part, :]
                plus = pltpu.roll(q, width - 1, 1)
                minus = pltpu.roll(q, 1, 1)
                stp[f, r + 1, part, :] = wendroff(q, half, half_square, plus, minus)

    def halo(way):
        source, target = (rows, 0) if way == 0 else (1, rows + 1)
        return pltpu.make_async_remote_copy(
            src_ref=stp.at[:, source],
            dst_ref=stp.at[:, target],
            send_sem=halo_send.at[way],
            recv_sem=halo_recv.at[way],
            device_id={"lat": lax.rem(lat + (1 if way == 0 else n_lat - 1), n_lat)},
            device_id_type=MESH,
        )

    has_next = lat < n_lat - 1
    has_last = lat > 0

    landed(fbuf, in_sem)

    @pl.loop(0, rows)
    def _(r):
        lon_row(r)

    def picked(group):
        return pl.ds(0, count) if group is None else span(group, LEAD)

    def slot(r, b, group):
        if group is None:
            return (r - 1) * per_row + b
        return whole * per_row + group * tail + lax.rem(r + SPLIT - 1, rows) * per_row + b

    def piece_copy(r, b, target, group):
        return pltpu.make_async_remote_copy(
            src_ref=sbuf.at[target, r, b, picked(group)],
            dst_ref=rbuf.at[r, b, picked(group), span(lev, depth)],
            send_sem=send_sem,
            recv_sem=recv_sem.at[slot(r, b, group)],
            device_id={"lev": target},
            device_id_type=MESH,
        )

    def wait_piece(r, b, group=None):
        landed(rbuf.at[r, b, picked(group)], recv_sem.at[slot(r, b, group)])

    def lat_row(r):
        @pl.loop(0, depth // 8)
        def _(g):
            part = span(g, 8)
            c = fbuf[count + 1, r, part, :]
            half, half_square = 0.5 * c, 0.5 * c * c
            for f in range(count):
                moved = wendroff(
                    stp[f, r + 1, part, :], half, half_square,
                    stp[f, r + 2, part, :], stp[f, r, part, :],
                )
                for p in range(n_lev):
                    for b in range(per_row):
                        at = p * piece + b * BLOCK_COLS
                        sbuf[p, r, b, f, part, :] = moved[:, at:at + BLOCK_COLS]

    def send_row(r, group=None):
        for b in range(per_row):
            for target in peers[-1:] + peers[:-1]:
                piece_copy(r, b, target, group).start()
        for b in range(per_row):
            pltpu.make_async_copy(
                sbuf.at[lev, r, b, picked(group)],
                rbuf.at[r, b, picked(group), span(lev, depth)],
                recv_sem.at[slot(r, b, group)],
            ).start()

    @pl.loop(1, whole + 1)
    def _(r):
        lat_row(r)
        send_row(r)

    for r in range(whole + 1, rows - 1):
        lat_row(r)
        send_row(r, 0)

    wait_for_lat()

    @pl.when(has_next)
    def _():
        halo(0).start()

    @pl.when(has_last)
    def _():
        halo(1).start()

    @pl.when(jnp.logical_not(has_last))
    def _():
        stp[:, 0] = jnp.zeros((count, depth, width), jnp.float32)

    @pl.when(jnp.logical_not(has_next))
    def _():
        stp[:, rows + 1] = jnp.zeros((count, depth, width), jnp.float32)

    for copy in small_loads:
        copy.wait()
    line = lax.broadcasted_iota(jnp.int32, (levels, levels), 0)
    column = lax.broadcasted_iota(jnp.int32, (levels, levels), 1)
    sun = jnp.sum(
        jnp.where(line == column, jnp.broadcast_to(sunbuf[...], (levels, levels)), 0.0),
        axis=1, keepdims=True,
    )
    triangle = (line >= column).astype(jnp.float32)
    lanes = lax.broadcasted_iota(jnp.int32, (1, BLOCK_COLS), 1)
    shares[...] = jnp.zeros_like(shares)

    landed(tbuf, thick_recv)

    @pl.loop(0, rows)
    def _(r):
        edge = jnp.dot(triangle, tbuf[r], precision=HIGH, preferred_element_type=jnp.float32)
        for b in range(per_row):
            cols = slice(b * BLOCK_COLS, (b + 1) * BLOCK_COLS)
            upper[r, b] = edge[:, cols]

    def spacing_of(r, b):
        return upper[r, b, levels - 1:levels, :] / levels

    def remap_block(r, b, base, some):
        cols = span(b, BLOCK_COLS)

        def put(f, i, tile):
            out[base + f, r, i:i + TILE, cols] = tile

        remap(
            levels, spacing_of(r, b), lambda j, k: upper[r, b, j:k, :],
            lambda f, j, k: rbuf[r, b, base + f, j:k, :], some, put, slope, above,
        )

    def heat_block(r, b):
        cols = span(b, BLOCK_COLS)
        temp, humid = out[0, r, :, cols], out[1, r, :, cols]
        square = humid * humid
        clear = 1.0 / (1.0 + square)
        heat = jnp.dot(
            jnp.concatenate([matrix[k] for k in range(matrix.shape[0])], axis=1),
            jnp.concatenate([square * clear * temp, clear * temp], axis=0),
            precision=HIGH, preferred_element_type=jnp.float32,
        )
        block = r * per_row + b
        warm = heat + day_of[block].astype(jnp.float32) * sun * clear
        heating[r, :, cols] = warm
        mean = jnp.sum(jnp.sum(warm, axis=0, keepdims=True), axis=1, keepdims=True)
        mean = mean * (1.0 / (levels * BLOCK_COLS))
        shares[...] = shares[...] + jnp.where(lanes == owner_of[block], mean, 0.0)

    def share_copy(d):
        return pltpu.make_async_remote_copy(
            src_ref=shares,
            dst_ref=gathered.at[d],
            send_sem=share_send,
            recv_sem=share_recv,
            device_id={"lat": lax.rem(lat + d, n_lat)},
            device_id_type=MESH,
        )

    @pl.loop(0, whole * per_row)
    def _(c):
        b = lax.rem(c, per_row)
        r = c // per_row + 1

        @pl.when(c == min(3, whole - 1) * per_row)
        def _():
            @pl.when(has_last)
            def _():
                halo(0).wait_recv()

            @pl.when(has_next)
            def _():
                halo(1).wait_recv()

            lat_row(rows - 1)
            send_row(rows - 1, 0)
            lat_row(0)
            send_row(0, 0)
            for group in range(1, groups):
                for k in range(SPLIT):
                    send_row((whole + 1 + k) % rows, group)

        wait_piece(r, b)
        remap_block(r, b, 0, count)
        heat_block(r, b)

    def tail_block(t):
        at = lax.rem(t, tail)
        return lax.rem(whole + 1 + at // per_row, rows), lax.rem(at, per_row), t // tail

    @pl.loop(0, groups * tail - 1)
    def _(t):
        r, b, group = tail_block(t)

        wait_piece(r, b, group)
        remap_block(r, b, group * LEAD, LEAD)

        @pl.when(group == 0)
        def _():
            heat_block(r, b)

        @pl.when(t == tail - 1)
        def _():
            @pl.loop(1, n_lat)
            def _(d):
                share_copy(d).start()

    end = per_row - 1
    carried[0:levels] = upper[0, end]

    landed(tbuf.at[:, pl.ds(0, depth * (n_lev - 1))], thick_send)

    @pl.when(has_next)
    def _():
        halo(0).wait_send()

    @pl.when(has_last)
    def _():
        halo(1).wait_send()

    others = gathered.at[pl.ds(1, n_lat - 1)]
    landed(others, share_recv)
    total = lax.fori_loop(1, n_lat, lambda d, total: total + gathered[d], shares[...])
    own = jnp.sum(jnp.where(lanes == lat, total, 0.0), axis=1, keepdims=True)
    carried[levels:] = jnp.broadcast_to(own, (8, BLOCK_COLS))
    landed(others, share_send)

    landed(sbuf.at[pl.ds(0, n_lev - 1)], send_sem)

    wait_piece(0, end, groups - 1)
    final[...] = rbuf[0, end, (groups - 1) * LEAD:groups * LEAD]


def store(
    moved, warm, final, carried, out, heating, owner_heat, tile, slope, above, owner, sems,
):
    count, rows, levels, piece = moved.shape
    rest = piece - BLOCK_COLS
    kept = count - LEAD
    owner[...] = carried[levels:levels + 1, 0:1]
    inner = pl.ds(1, rows - 1)
    pairs = [
        (moved.at[:, inner], out.at[:, inner]),
        (warm, heating),
        (owner, owner_heat),
        (moved.at[pl.ds(0, kept), 0], out.at[pl.ds(0, kept), 0]),
    ]
    if rest:
        pairs.append((
            moved.at[pl.ds(kept, LEAD), 0, :, pl.ds(0, rest)],
            out.at[pl.ds(kept, LEAD), 0, :, pl.ds(0, rest)],
        ))
    copies = [
        pltpu.make_async_copy(source, target, sems.at[k])
        for k, (source, target) in enumerate(pairs)
    ]
    for copy in copies:
        copy.start()

    def put(f, i, value):
        tile[f, i:i + TILE, :] = value

    remap(
        levels, carried[levels - 1:levels, :] / levels, lambda j, k: carried[j:k, :],
        lambda f, j, k: final[f, j:k, :], LEAD, put, slope, above,
    )
    last = pltpu.make_async_copy(
        tile, out.at[pl.ds(kept, LEAD), 0, :, pl.ds(rest, BLOCK_COLS)], sems.at[len(pairs)]
    )
    last.start()
    for copy in copies:
        copy.wait()
    last.wait()


def per_device(
    fields, thickness, courant_lon, courant_lat, exchange, solar_profile, owners, daylight
):
    n_lat, n_lev = lax.axis_size("lat"), lax.axis_size("lev")
    count, rows, depth, width = fields.shape
    levels = solar_profile.shape[0]
    piece = width // n_lev
    per_row = piece // BLOCK_COLS
    groups = count // LEAD
    f32 = jnp.float32
    dma = pltpu.SemaphoreType.DMA
    regular = pltpu.SemaphoreType.REGULAR
    hbm = pl.BlockSpec(memory_space=pltpu.HBM)
    vmem = pl.BlockSpec(memory_space=pltpu.VMEM)
    moved = jax.ShapeDtypeStruct((count, rows, levels, piece), f32)
    warm = jax.ShapeDtypeStruct((rows, levels, piece), f32)
    owner = jax.ShapeDtypeStruct((1, 1), f32)
    results = pl.pallas_call(
        functools.partial(kernel, n_lat, n_lev),
        out_shape=(
            pltpu.VMEM(moved.shape, f32),
            pltpu.VMEM(warm.shape, f32),
            pltpu.VMEM((LEAD, levels, BLOCK_COLS), f32),
            pltpu.VMEM((levels + 8, BLOCK_COLS), f32),
        ),
        in_specs=[hbm] * 8,
        out_specs=(vmem,) * 4,
        scratch_shapes=[
            pltpu.VMEM((count + 2, rows, depth, width), f32),
            pltpu.VMEM((count, rows + 2, depth, width), f32),
            pltpu.VMEM((n_lev, rows, per_row, count, depth, BLOCK_COLS), f32),
            pltpu.VMEM((rows, per_row, count, levels, BLOCK_COLS), f32),
            pltpu.VMEM((rows, levels, piece), f32),
            pltpu.VMEM(exchange.shape, f32),
            pltpu.VMEM((1, levels), f32),
            pltpu.VMEM((rows, per_row, levels, BLOCK_COLS), f32),
            pltpu.VMEM((count, levels, BLOCK_COLS), f32),
            pltpu.VMEM((levels, BLOCK_COLS), f32),
            pltpu.VMEM((1, BLOCK_COLS), f32),
            pltpu.VMEM((n_lat, 1, BLOCK_COLS), f32),
            pltpu.SMEM((rows * per_row,), jnp.int32),
            pltpu.SMEM((rows * per_row,), jnp.int32),
            regular,
            dma,
            dma((4,)),
            dma((2,)),
            dma((2,)),
            dma,
            dma,
            dma,
            dma(((rows - SPLIT + SPLIT * groups) * per_row,)),
            dma,
            dma,
        ],
        compiler_params=pltpu.CompilerParams(
            collective_id=0, has_side_effects=True, vmem_limit_bytes=61400000
        ),
    )(
        fields, thickness, courant_lon, courant_lat, exchange, solar_profile[None, :],
        owners[:, 0], daylight,
    )
    return pl.pallas_call(
        store,
        out_shape=(moved, warm, owner),
        in_specs=[vmem] * 4,
        out_specs=(hbm,) * 3,
        scratch_shapes=[
            pltpu.VMEM((LEAD, levels, BLOCK_COLS), f32),
            pltpu.VMEM((LEAD, levels, BLOCK_COLS), f32),
            pltpu.VMEM((levels, BLOCK_COLS), f32),
            pltpu.VMEM(owner.shape, f32),
            dma((6,)),
        ],
        compiler_params=pltpu.CompilerParams(vmem_limit_bytes=12 * 1024 * 1024),
    )(*results)


def solution(mesh):
    placed = (
        P(None, "lat", "lev", None),
        P("lat", "lev", None),
        P("lat", "lev", None),
        P("lat", "lev", None),
        P(),
        P(),
        P(("lat", "lev"), None),
        P(("lat", "lev")),
    )
    return jax.shard_map(
        per_device,
        mesh=mesh,
        in_specs=placed,
        out_specs=(P(None, "lat", None, "lev"), P("lat", None, "lev"), P("lat", "lev")),
        check_vma=False,
    )
```

```python
import functools

import jax
import jax.numpy as jnp
from jax import lax
from jax.experimental import pallas as pl
from jax.experimental.pallas import tpu as pltpu
from jax.sharding import PartitionSpec as P

BLOCK_COLS = 128
THIN, THICK = 0.5, 1.5
TILE = 16
STEP = 4
LONG = 8
LEAD = 2
SPLIT = 3
HIGH = lax.Precision.HIGHEST
MESH = pl.DeviceIdType.MESH


def wendroff(values, half, half_square, plus, minus):
    return values - half * (plus - minus) + half_square * (plus - 2.0 * values + minus)


def layers_of(first, last, levels):
    def most(n):
        return levels * THICK * n / (THICK * n + THIN * (levels - n))

    def least(n):
        return levels * THIN * n / (THIN * n + THICK * (levels - n))

    slack = 0.01
    hit = [j for j in range(levels) if least(j + 1) < last + slack and most(j + 1) > first - slack]
    return hit[0] // STEP * STEP, min(levels, -(-(hit[-1] + 1) // STEP) * STEP)


def remap(levels, spacing, edges, values, count, put, slope, above):
    inverse = 1.0 / spacing
    row = lax.broadcasted_iota(jnp.int32, (TILE, BLOCK_COLS), 0)
    rise = (row + 1).astype(jnp.float32) * spacing
    top = levels - 8
    for f in range(count):
        slope[f, 0:top] = values(f, 0, top) - values(f, 1, top + 1)
        q = values(f, top, levels)
        slope[f, top:levels] = q - jnp.where(row[:8] == 7, 0.0, pltpu.roll(q, 7, 0))
    for i in range(0, levels, TILE):
        first, last = layers_of(i, i + TILE, levels)
        base = spacing * float(i)
        start, stop = first // 8 * 8, -(-last // 8) * 8
        above[start:stop] = jnp.maximum(edges(start, stop), base) - base

        def add(j0, steps, sums):
            for s in range(steps):
                j = pl.ds(j0 + s, 1)
                reach = jnp.minimum(rise, above[j, :])
                sums = tuple(total + reach * slope[f, j, :] for f, total in enumerate(sums))
            return sums

        def add_long(g, sums, add=add, first=first):
            return add(first + g * LONG, LONG, sums)

        trips, rest = divmod(last - first, LONG)
        if last < levels:
            sums = tuple(rise * values(f, last, last + 1) for f in range(count))
        else:
            sums = (jnp.zeros((TILE, BLOCK_COLS), jnp.float32),) * count
        sums = lax.fori_loop(0, trips, add_long, sums)
        if rest:
            sums = add(last - rest, rest, sums)
        for f, total in enumerate(sums):
            below = jnp.where(row == 0, 0.0, pltpu.roll(total, 1, 0))
            put(f, i, (total - below) * inverse)


def kernel(
    n_lat, n_lev,
    fields, thickness, courant_lon, courant_lat, exchange, solar, owners, daylight,
    out, heating, final, carried,
    fbuf, stp, sbuf, rbuf, tbuf, matrix, sunbuf, upper, slope, above, shares, gathered,
    owner_of, day_of, word,
    in_sem, small_sem, halo_send, halo_recv, thick_send, thick_recv,
    send_sem, recv_sem, share_send, share_recv,
):
    count, rows, depth, width = fields.shape
    levels = out.shape[2]
    piece = width // n_lev
    per_row = piece // BLOCK_COLS
    groups = count // LEAD
    whole = rows - SPLIT
    tail = SPLIT * per_row
    lat = lax.axis_index("lat")
    lev = lax.axis_index("lev")
    odd = lax.rem(lev, 2) == 1
    even = jnp.logical_not(odd)
    partner = lev + 1 - 2 * lax.rem(lev, 2)

    barrier = pltpu.get_barrier_semaphore()
    for d in range(1, n_lev):
        peer = lax.rem(lev + d, n_lev)

        @pl.when(lax.rem(peer, 2) == 0)
        def _():
            pl.semaphore_signal(barrier, inc=1, device_id={"lev": peer}, device_id_type=MESH)

    def span(index, size):
        return pl.ds(pl.multiple_of(index * size, size), size)

    def landed(buffer, sem):
        pltpu.make_async_copy(buffer, buffer, sem).wait()

    @pl.when(even)
    def _():
        pl.semaphore_wait(barrier, n_lev - 1)
        pl.semaphore_signal(word, inc=1, device_id={"lev": partner}, device_id_type=MESH)

    @pl.when(odd)
    def _():
        pl.semaphore_wait(word, 1)

    def wait_for_lat():
        @pl.when(odd)
        def _():
            pl.semaphore_wait(barrier, n_lat - 1)
            pl.semaphore_signal(word, inc=1, device_id={"lev": partner}, device_id_type=MESH)

        @pl.when(even)
        def _():
            pl.semaphore_wait(word, 1)

    first = lev - lax.rem(lev, 2)
    peers = [lax.rem(first + d, n_lev) for d in range(2, n_lev)] + [partner]

    for target in peers:
        pltpu.make_async_remote_copy(
            src_ref=thickness.at[:, :, span(target, piece)],
            dst_ref=tbuf.at[:, span(lev, depth)],
            send_sem=thick_send,
            recv_sem=thick_recv,
            device_id={"lev": target},
            device_id_type=MESH,
        ).start()
    pltpu.make_async_copy(fields, fbuf.at[pl.ds(0, count)], in_sem).start()
    pltpu.make_async_copy(courant_lon, fbuf.at[count], in_sem).start()
    pltpu.make_async_copy(courant_lat, fbuf.at[count + 1], in_sem).start()
    pltpu.make_async_copy(
        thickness.at[:, :, span(lev, piece)], tbuf.at[:, span(lev, depth)], thick_recv
    ).start()

    @pl.when(odd)
    def _():
        @pl.loop(1, n_lat)
        def _(d):
            pl.semaphore_signal(
                barrier, inc=1, device_id={"lat": lax.rem(lat + d, n_lat)}, device_id_type=MESH
            )

    small = ((exchange, matrix), (solar, sunbuf), (owners, owner_of), (daylight, day_of))
    small_loads = [
        pltpu.make_async_copy(source, target, small_sem.at[k])
        for k, (source, target) in enumerate(small)
    ]
    for copy in small_loads:
        copy.start()

    def lon_row(r):
        @pl.loop(0, depth // 8)
        def _(g):
            part = span(g, 8)
            c = fbuf[count, r, part, :]
            half, half_square = 0.5 * c, 0.5 * c * c
            for f in range(count):
                q = fbuf[f, r, part, :]
                plus = pltpu.roll(q, width - 1, 1)
                minus = pltpu.roll(q, 1, 1)
                stp[f, r + 1, part, :] = wendroff(q, half, half_square, plus, minus)

    def halo(way):
        source, target = (rows, 0) if way == 0 else (1, rows + 1)
        return pltpu.make_async_remote_copy(
            src_ref=stp.at[:, source],
            dst_ref=stp.at[:, target],
            send_sem=halo_send.at[way],
            recv_sem=halo_recv.at[way],
            device_id={"lat": lax.rem(lat + (1 if way == 0 else n_lat - 1), n_lat)},
            device_id_type=MESH,
        )

    has_next = lat < n_lat - 1
    has_last = lat > 0

    landed(fbuf, in_sem)

    @pl.loop(0, rows)
    def _(r):
        lon_row(r)

    def picked(group):
        return pl.ds(0, count) if group is None else span(group, LEAD)

    def slot(r, b, group):
        if group is None:
            return (r - 1) * per_row + b
        return whole * per_row + group * tail + lax.rem(r + SPLIT - 1, rows) * per_row + b

    def piece_copy(r, b, target, group):
        return pltpu.make_async_remote_copy(
            src_ref=sbuf.at[target, r, b, picked(group)],
            dst_ref=rbuf.at[r, b, picked(group), span(lev, depth)],
            send_sem=send_sem,
            recv_sem=recv_sem.at[slot(r, b, group)],
            device_id={"lev": target},
            device_id_type=MESH,
        )

    def wait_piece(r, b, group=None):
        landed(rbuf.at[r, b, picked(group)], recv_sem.at[slot(r, b, group)])

    def lat_row(r):
        @pl.loop(0, depth // 8)
        def _(g):
            part = span(g, 8)
            c = fbuf[count + 1, r, part, :]
            half, half_square = 0.5 * c, 0.5 * c * c
            for f in range(count):
                moved = wendroff(
                    stp[f, r + 1, part, :], half, half_square,
                    stp[f, r + 2, part, :], stp[f, r, part, :],
                )
                for p in range(n_lev):
                    for b in range(per_row):
                        at = p * piece + b * BLOCK_COLS
                        sbuf[p, r, b, f, part, :] = moved[:, at:at + BLOCK_COLS]

    def send_row(r, group=None):
        for b in range(per_row):
            for target in peers[-1:] + peers[:-1]:
                piece_copy(r, b, target, group).start()
        for b in range(per_row):
            pltpu.make_async_copy(
                sbuf.at[lev, r, b, picked(group)],
                rbuf.at[r, b, picked(group), span(lev, depth)],
                recv_sem.at[slot(r, b, group)],
            ).start()

    @pl.loop(1, whole + 1)
    def _(r):
        lat_row(r)
        send_row(r)

    for r in range(whole + 1, rows - 1):
        lat_row(r)
        send_row(r, 0)

    wait_for_lat()

    @pl.when(has_next)
    def _():
        halo(0).start()

    @pl.when(has_last)
    def _():
        halo(1).start()

    @pl.when(jnp.logical_not(has_last))
    def _():
        stp[:, 0] = jnp.zeros((count, depth, width), jnp.float32)

    @pl.when(jnp.logical_not(has_next))
    def _():
        stp[:, rows + 1] = jnp.zeros((count, depth, width), jnp.float32)

    for copy in small_loads:
        copy.wait()
    line = lax.broadcasted_iota(jnp.int32, (levels, levels), 0)
    column = lax.broadcasted_iota(jnp.int32, (levels, levels), 1)
    sun = jnp.sum(
        jnp.where(line == column, jnp.broadcast_to(sunbuf[...], (levels, levels)), 0.0),
        axis=1, keepdims=True,
    )
    triangle = (line >= column).astype(jnp.float32)
    lanes = lax.broadcasted_iota(jnp.int32, (1, BLOCK_COLS), 1)
    shares[...] = jnp.zeros_like(shares)

    landed(tbuf, thick_recv)

    @pl.loop(0, rows)
    def _(r):
        edge = jnp.dot(triangle, tbuf[r], precision=HIGH, preferred_element_type=jnp.float32)
        for b in range(per_row):
            cols = slice(b * BLOCK_COLS, (b + 1) * BLOCK_COLS)
            upper[r, b] = edge[:, cols]

    def spacing_of(r, b):
        return upper[r, b, levels - 1:levels, :] / levels

    def remap_block(r, b, base, some):
        cols = span(b, BLOCK_COLS)

        def put(f, i, tile):
            out[base + f, r, i:i + TILE, cols] = tile

        remap(
            levels, spacing_of(r, b), lambda j, k: upper[r, b, j:k, :],
            lambda f, j, k: rbuf[r, b, base + f, j:k, :], some, put, slope, above,
        )

    def heat_block(r, b):
        cols = span(b, BLOCK_COLS)
        temp, humid = out[0, r, :, cols], out[1, r, :, cols]
        square = humid * humid
        clear = 1.0 / (1.0 + square)
        heat = jnp.dot(
            jnp.concatenate([matrix[k] for k in range(matrix.shape[0])], axis=1),
            jnp.concatenate([square * clear * temp, clear * temp], axis=0),
            precision=HIGH, preferred_element_type=jnp.float32,
        )
        block = r * per_row + b
        warm = heat + day_of[block].astype(jnp.float32) * sun * clear
        heating[r, :, cols] = warm
        mean = jnp.sum(jnp.sum(warm, axis=0, keepdims=True), axis=1, keepdims=True)
        mean = mean * (1.0 / (levels * BLOCK_COLS))
        shares[...] = shares[...] + jnp.where(lanes == owner_of[block], mean, 0.0)

    def share_copy(d):
        return pltpu.make_async_remote_copy(
            src_ref=shares,
            dst_ref=gathered.at[d],
            send_sem=share_send,
            recv_sem=share_recv,
            device_id={"lat": lax.rem(lat + d, n_lat)},
            device_id_type=MESH,
        )

    @pl.loop(0, whole * per_row)
    def _(c):
        b = lax.rem(c, per_row)
        r = c // per_row + 1

        @pl.when(c == min(4, whole - 1) * per_row)
        def _():
            @pl.when(has_last)
            def _():
                halo(0).wait_recv()

            @pl.when(has_next)
            def _():
                halo(1).wait_recv()

            lat_row(rows - 1)
            send_row(rows - 1, 0)
            lat_row(0)
            send_row(0, 0)
            for group in range(1, groups):
                for k in range(SPLIT):
                    send_row((whole + 1 + k) % rows, group)

        wait_piece(r, b)
        remap_block(r, b, 0, count)
        heat_block(r, b)

    def tail_block(t):
        at = lax.rem(t, tail)
        return lax.rem(whole + 1 + at // per_row, rows), lax.rem(at, per_row), t // tail

    @pl.loop(0, groups * tail - 1)
    def _(t):
        r, b, group = tail_block(t)

        wait_piece(r, b, group)
        remap_block(r, b, group * LEAD, LEAD)

        @pl.when(group == 0)
        def _():
            heat_block(r, b)

        @pl.when(t == tail - 1)
        def _():
            @pl.loop(1, n_lat)
            def _(d):
                share_copy(d).start()

    end = per_row - 1
    carried[0:levels] = upper[0, end]

    landed(tbuf.at[:, pl.ds(0, depth * (n_lev - 1))], thick_send)

    @pl.when(has_next)
    def _():
        halo(0).wait_send()

    @pl.when(has_last)
    def _():
        halo(1).wait_send()

    others = gathered.at[pl.ds(1, n_lat - 1)]
    landed(others, share_recv)
    total = lax.fori_loop(1, n_lat, lambda d, total: total + gathered[d], shares[...])
    own = jnp.sum(jnp.where(lanes == lat, total, 0.0), axis=1, keepdims=True)
    carried[levels:] = jnp.broadcast_to(own, (8, BLOCK_COLS))
    landed(others, share_send)

    landed(sbuf.at[pl.ds(0, n_lev - 1)], send_sem)

    wait_piece(0, end, groups - 1)
    final[...] = rbuf[0, end, (groups - 1) * LEAD:groups * LEAD]


def store(
    moved, warm, final, carried, out, heating, owner_heat, tile, slope, above, owner, sems,
):
    count, rows, levels, piece = moved.shape
    rest = piece - BLOCK_COLS
    kept = count - LEAD
    owner[...] = carried[levels:levels + 1, 0:1]
    inner = pl.ds(1, rows - 1)
    pairs = [
        (moved.at[:, inner], out.at[:, inner]),
        (warm, heating),
        (owner, owner_heat),
        (moved.at[pl.ds(0, kept), 0], out.at[pl.ds(0, kept), 0]),
    ]
    if rest:
        pairs.append((
            moved.at[pl.ds(kept, LEAD), 0, :, pl.ds(0, rest)],
            out.at[pl.ds(kept, LEAD), 0, :, pl.ds(0, rest)],
        ))
    copies = [
        pltpu.make_async_copy(source, target, sems.at[k])
        for k, (source, target) in enumerate(pairs)
    ]
    for copy in copies:
        copy.start()

    def put(f, i, value):
        tile[f, i:i + TILE, :] = value

    remap(
        levels, carried[levels - 1:levels, :] / levels, lambda j, k: carried[j:k, :],
        lambda f, j, k: final[f, j:k, :], LEAD, put, slope, above,
    )
    last = pltpu.make_async_copy(
        tile, out.at[pl.ds(kept, LEAD), 0, :, pl.ds(rest, BLOCK_COLS)], sems.at[len(pairs)]
    )
    last.start()
    for copy in copies:
        copy.wait()
    last.wait()


def per_device(
    fields, thickness, courant_lon, courant_lat, exchange, solar_profile, owners, daylight
):
    n_lat, n_lev = lax.axis_size("lat"), lax.axis_size("lev")
    count, rows, depth, width = fields.shape
    levels = solar_profile.shape[0]
    piece = width // n_lev
    per_row = piece // BLOCK_COLS
    groups = count // LEAD
    f32 = jnp.float32
    dma = pltpu.SemaphoreType.DMA
    regular = pltpu.SemaphoreType.REGULAR
    hbm = pl.BlockSpec(memory_space=pltpu.HBM)
    vmem = pl.BlockSpec(memory_space=pltpu.VMEM)
    moved = jax.ShapeDtypeStruct((count, rows, levels, piece), f32)
    warm = jax.ShapeDtypeStruct((rows, levels, piece), f32)
    owner = jax.ShapeDtypeStruct((1, 1), f32)
    results = pl.pallas_call(
        functools.partial(kernel, n_lat, n_lev),
        out_shape=(
            pltpu.VMEM(moved.shape, f32),
            pltpu.VMEM(warm.shape, f32),
            pltpu.VMEM((LEAD, levels, BLOCK_COLS), f32),
            pltpu.VMEM((levels + 8, BLOCK_COLS), f32),
        ),
        in_specs=[hbm] * 8,
        out_specs=(vmem,) * 4,
        scratch_shapes=[
            pltpu.VMEM((count + 2, rows, depth, width), f32),
            pltpu.VMEM((count, rows + 2, depth, width), f32),
            pltpu.VMEM((n_lev, rows, per_row, count, depth, BLOCK_COLS), f32),
            pltpu.VMEM((rows, per_row, count, levels, BLOCK_COLS), f32),
            pltpu.VMEM((rows, levels, piece), f32),
            pltpu.VMEM(exchange.shape, f32),
            pltpu.VMEM((1, levels), f32),
            pltpu.VMEM((rows, per_row, levels, BLOCK_COLS), f32),
            pltpu.VMEM((count, levels, BLOCK_COLS), f32),
            pltpu.VMEM((levels, BLOCK_COLS), f32),
            pltpu.VMEM((1, BLOCK_COLS), f32),
            pltpu.VMEM((n_lat, 1, BLOCK_COLS), f32),
            pltpu.SMEM((rows * per_row,), jnp.int32),
            pltpu.SMEM((rows * per_row,), jnp.int32),
            regular,
            dma,
            dma((4,)),
            dma((2,)),
            dma((2,)),
            dma,
            dma,
            dma,
            dma(((rows - SPLIT + SPLIT * groups) * per_row,)),
            dma,
            dma,
        ],
        compiler_params=pltpu.CompilerParams(
            collective_id=0, has_side_effects=True, vmem_limit_bytes=61400000
        ),
    )(
        fields, thickness, courant_lon, courant_lat, exchange, solar_profile[None, :],
        owners[:, 0], daylight,
    )
    return pl.pallas_call(
        store,
        out_shape=(moved, warm, owner),
        in_specs=[vmem] * 4,
        out_specs=(hbm,) * 3,
        scratch_shapes=[
            pltpu.VMEM((LEAD, levels, BLOCK_COLS), f32),
            pltpu.VMEM((LEAD, levels, BLOCK_COLS), f32),
            pltpu.VMEM((levels, BLOCK_COLS), f32),
            pltpu.VMEM(owner.shape, f32),
            dma((6,)),
        ],
        compiler_params=pltpu.CompilerParams(vmem_limit_bytes=12 * 1024 * 1024),
    )(*results)


def solution(mesh):
    placed = (
        P(None, "lat", "lev", None),
        P("lat", "lev", None),
        P("lat", "lev", None),
        P("lat", "lev", None),
        P(),
        P(),
        P(("lat", "lev"), None),
        P(("lat", "lev")),
    )
    return jax.shard_map(
        per_device,
        mesh=mesh,
        in_specs=placed,
        out_specs=(P(None, "lat", None, "lev"), P("lat", None, "lev"), P("lat", "lev")),
        check_vma=False,
    )
```

```python
import functools

import jax
import jax.numpy as jnp
from jax import lax
from jax.experimental import pallas as pl
from jax.experimental.pallas import tpu as pltpu
from jax.sharding import PartitionSpec as P

BLOCK_COLS = 128
THIN, THICK = 0.5, 1.5
TILE = 16
STEP = 4
LONG = 8
LEAD = 2
SPLIT = 3
HIGH = lax.Precision.HIGHEST
MESH = pl.DeviceIdType.MESH


def wendroff(values, half, half_square, plus, minus):
    return values - half * (plus - minus) + half_square * (plus - 2.0 * values + minus)


def layers_of(first, last, levels):
    def most(n):
        return levels * THICK * n / (THICK * n + THIN * (levels - n))

    def least(n):
        return levels * THIN * n / (THIN * n + THICK * (levels - n))

    slack = 0.01
    hit = [j for j in range(levels) if least(j + 1) < last + slack and most(j + 1) > first - slack]
    return hit[0] // STEP * STEP, min(levels, -(-(hit[-1] + 1) // STEP) * STEP)


def remap(levels, spacing, edges, values, count, put, slope, above):
    inverse = 1.0 / spacing
    row = lax.broadcasted_iota(jnp.int32, (TILE, BLOCK_COLS), 0)
    rise = (row + 1).astype(jnp.float32) * spacing
    top = levels - 8
    for f in range(count):
        slope[f, 0:top] = values(f, 0, top) - values(f, 1, top + 1)
        q = values(f, top, levels)
        slope[f, top:levels] = q - jnp.where(row[:8] == 7, 0.0, pltpu.roll(q, 7, 0))
    for i in range(0, levels, TILE):
        first, last = layers_of(i, i + TILE, levels)
        base = spacing * float(i)
        start, stop = first // 8 * 8, -(-last // 8) * 8
        above[start:stop] = jnp.maximum(edges(start, stop), base) - base

        def add(j0, steps, sums):
            for s in range(steps):
                j = pl.ds(j0 + s, 1)
                reach = jnp.minimum(rise, above[j, :])
                sums = tuple(total + reach * slope[f, j, :] for f, total in enumerate(sums))
            return sums

        def add_long(g, sums, add=add, first=first):
            return add(first + g * LONG, LONG, sums)

        trips, rest = divmod(last - first, LONG)
        if last < levels:
            sums = tuple(rise * values(f, last, last + 1) for f in range(count))
        else:
            sums = (jnp.zeros((TILE, BLOCK_COLS), jnp.float32),) * count
        sums = lax.fori_loop(0, trips, add_long, sums)
        if rest:
            sums = add(last - rest, rest, sums)
        for f, total in enumerate(sums):
            below = jnp.where(row == 0, 0.0, pltpu.roll(total, 1, 0))
            put(f, i, (total - below) * inverse)


def kernel(
    n_lat, n_lev,
    fields, thickness, courant_lon, courant_lat, exchange, solar, owners, daylight,
    out, heating, final, carried,
    fbuf, stp, sbuf, rbuf, tbuf, matrix, triple, sunbuf, upper, slope, above, shares, gathered,
    owner_of, day_of, word,
    in_sem, small_sem, halo_send, halo_recv, thick_send, thick_recv,
    send_sem, recv_sem, share_send, share_recv,
):
    count, rows, depth, width = fields.shape
    levels = out.shape[2]
    piece = width // n_lev
    per_row = piece // BLOCK_COLS
    groups = count // LEAD
    whole = rows - SPLIT
    tail = SPLIT * per_row
    lat = lax.axis_index("lat")
    lev = lax.axis_index("lev")
    odd = lax.rem(lev, 2) == 1
    even = jnp.logical_not(odd)
    partner = lev + 1 - 2 * lax.rem(lev, 2)

    barrier = pltpu.get_barrier_semaphore()
    for d in range(1, n_lev):
        peer = lax.rem(lev + d, n_lev)

        @pl.when(lax.rem(peer, 2) == 0)
        def _():
            pl.semaphore_signal(barrier, inc=1, device_id={"lev": peer}, device_id_type=MESH)

    def span(index, size):
        return pl.ds(pl.multiple_of(index * size, size), size)

    def landed(buffer, sem):
        pltpu.make_async_copy(buffer, buffer, sem).wait()

    @pl.when(even)
    def _():
        pl.semaphore_wait(barrier, n_lev - 1)
        pl.semaphore_signal(word, inc=1, device_id={"lev": partner}, device_id_type=MESH)

    @pl.when(odd)
    def _():
        pl.semaphore_wait(word, 1)

    def wait_for_lat():
        @pl.when(odd)
        def _():
            pl.semaphore_wait(barrier, n_lat - 1)
            pl.semaphore_signal(word, inc=1, device_id={"lev": partner}, device_id_type=MESH)

        @pl.when(even)
        def _():
            pl.semaphore_wait(word, 1)

    first = lev - lax.rem(lev, 2)
    peers = [lax.rem(first + d, n_lev) for d in range(2, n_lev)] + [partner]

    def halves(x):
        high = x.astype(jnp.bfloat16)
        return high, (x - high.astype(jnp.float32)).astype(jnp.bfloat16)

    for target in peers:
        pltpu.make_async_remote_copy(
            src_ref=thickness.at[:, :, span(target, piece)],
            dst_ref=tbuf.at[:, span(lev, depth)],
            send_sem=thick_send,
            recv_sem=thick_recv,
            device_id={"lev": target},
            device_id_type=MESH,
        ).start()
    pltpu.make_async_copy(fields, fbuf.at[pl.ds(0, count)], in_sem).start()
    pltpu.make_async_copy(courant_lon, fbuf.at[count], in_sem).start()
    pltpu.make_async_copy(courant_lat, fbuf.at[count + 1], in_sem).start()
    pltpu.make_async_copy(
        thickness.at[:, :, span(lev, piece)], tbuf.at[:, span(lev, depth)], thick_recv
    ).start()

    @pl.when(odd)
    def _():
        @pl.loop(1, n_lat)
        def _(d):
            pl.semaphore_signal(
                barrier, inc=1, device_id={"lat": lax.rem(lat + d, n_lat)}, device_id_type=MESH
            )

    small = ((exchange, matrix), (solar, sunbuf), (owners, owner_of), (daylight, day_of))
    small_loads = [
        pltpu.make_async_copy(source, target, small_sem.at[k])
        for k, (source, target) in enumerate(small)
    ]
    for copy in small_loads:
        copy.start()

    def lon_row(r):
        @pl.loop(0, depth // 8)
        def _(g):
            part = span(g, 8)
            c = fbuf[count, r, part, :]
            half, half_square = 0.5 * c, 0.5 * c * c
            for f in range(count):
                q = fbuf[f, r, part, :]
                plus = pltpu.roll(q, width - 1, 1)
                minus = pltpu.roll(q, 1, 1)
                stp[f, r + 1, part, :] = wendroff(q, half, half_square, plus, minus)

    def halo(way):
        source, target = (rows, 0) if way == 0 else (1, rows + 1)
        return pltpu.make_async_remote_copy(
            src_ref=stp.at[:, source],
            dst_ref=stp.at[:, target],
            send_sem=halo_send.at[way],
            recv_sem=halo_recv.at[way],
            device_id={"lat": lax.rem(lat + (1 if way == 0 else n_lat - 1), n_lat)},
            device_id_type=MESH,
        )

    has_next = lat < n_lat - 1
    has_last = lat > 0

    landed(fbuf, in_sem)

    @pl.loop(0, rows)
    def _(r):
        lon_row(r)

    def picked(group):
        return pl.ds(0, count) if group is None else span(group, LEAD)

    def slot(r, b, group):
        if group is None:
            return (r - 1) * per_row + b
        return whole * per_row + group * tail + lax.rem(r + SPLIT - 1, rows) * per_row + b

    def piece_copy(r, b, target, group):
        return pltpu.make_async_remote_copy(
            src_ref=sbuf.at[target, r, b, picked(group)],
            dst_ref=rbuf.at[r, b, picked(group), span(lev, depth)],
            send_sem=send_sem,
            recv_sem=recv_sem.at[slot(r, b, group)],
            device_id={"lev": target},
            device_id_type=MESH,
        )

    def wait_piece(r, b, group=None):
        landed(rbuf.at[r, b, picked(group)], recv_sem.at[slot(r, b, group)])

    def lat_row(r):
        @pl.loop(0, depth // 8)
        def _(g):
            part = span(g, 8)
            c = fbuf[count + 1, r, part, :]
            half, half_square = 0.5 * c, 0.5 * c * c
            for f in range(count):
                moved = wendroff(
                    stp[f, r + 1, part, :], half, half_square,
                    stp[f, r + 2, part, :], stp[f, r, part, :],
                )
                for p in range(n_lev):
                    for b in range(per_row):
                        at = p * piece + b * BLOCK_COLS
                        sbuf[p, r, b, f, part, :] = moved[:, at:at + BLOCK_COLS]

    def send_row(r, group=None):
        for b in range(per_row):
            for target in peers[-1:] + peers[:-1]:
                piece_copy(r, b, target, group).start()
        for b in range(per_row):
            pltpu.make_async_copy(
                sbuf.at[lev, r, b, picked(group)],
                rbuf.at[r, b, picked(group), span(lev, depth)],
                recv_sem.at[slot(r, b, group)],
            ).start()

    @pl.loop(1, whole + 1)
    def _(r):
        lat_row(r)
        send_row(r)

    for r in range(whole + 1, rows - 1):
        lat_row(r)
        send_row(r, 0)

    wait_for_lat()

    @pl.when(has_next)
    def _():
        halo(0).start()

    @pl.when(has_last)
    def _():
        halo(1).start()

    @pl.when(jnp.logical_not(has_last))
    def _():
        stp[:, 0] = jnp.zeros((count, depth, width), jnp.float32)

    @pl.when(jnp.logical_not(has_next))
    def _():
        stp[:, rows + 1] = jnp.zeros((count, depth, width), jnp.float32)

    for copy in small_loads:
        copy.wait()
    high, rest = halves(jnp.concatenate([matrix[k] for k in range(matrix.shape[0])], axis=1))
    triple[...] = jnp.concatenate([high, high, rest], axis=1)
    line = lax.broadcasted_iota(jnp.int32, (levels, levels), 0)
    column = lax.broadcasted_iota(jnp.int32, (levels, levels), 1)
    sun = jnp.sum(
        jnp.where(line == column, jnp.broadcast_to(sunbuf[...], (levels, levels)), 0.0),
        axis=1, keepdims=True,
    )
    triangle = (line >= column).astype(jnp.float32)
    lanes = lax.broadcasted_iota(jnp.int32, (1, BLOCK_COLS), 1)
    shares[...] = jnp.zeros_like(shares)

    landed(tbuf, thick_recv)

    @pl.loop(0, rows)
    def _(r):
        edge = jnp.dot(triangle, tbuf[r], precision=HIGH, preferred_element_type=jnp.float32)
        for b in range(per_row):
            cols = slice(b * BLOCK_COLS, (b + 1) * BLOCK_COLS)
            upper[r, b] = edge[:, cols]

    def spacing_of(r, b):
        return upper[r, b, levels - 1:levels, :] / levels

    def remap_block(r, b, base, some):
        cols = span(b, BLOCK_COLS)

        def put(f, i, tile):
            out[base + f, r, i:i + TILE, cols] = tile

        remap(
            levels, spacing_of(r, b), lambda j, k: upper[r, b, j:k, :],
            lambda f, j, k: rbuf[r, b, base + f, j:k, :], some, put, slope, above,
        )

    def heat_block(r, b):
        cols = span(b, BLOCK_COLS)
        temp, humid = out[0, r, :, cols], out[1, r, :, cols]
        square = humid * humid
        clear = 1.0 / (1.0 + square)
        high, rest = halves(jnp.concatenate([square * clear * temp, clear * temp], axis=0))
        heat = jnp.dot(
            triple[...], jnp.concatenate([high, rest, high], axis=0),
            preferred_element_type=jnp.float32,
        )
        block = r * per_row + b
        warm = heat + day_of[block].astype(jnp.float32) * sun * clear
        heating[r, :, cols] = warm
        mean = jnp.sum(jnp.sum(warm, axis=0, keepdims=True), axis=1, keepdims=True)
        mean = mean * (1.0 / (levels * BLOCK_COLS))
        shares[...] = shares[...] + jnp.where(lanes == owner_of[block], mean, 0.0)

    def share_copy(d):
        return pltpu.make_async_remote_copy(
            src_ref=shares,
            dst_ref=gathered.at[d],
            send_sem=share_send,
            recv_sem=share_recv,
            device_id={"lat": lax.rem(lat + d, n_lat)},
            device_id_type=MESH,
        )

    @pl.loop(0, whole * per_row)
    def _(c):
        b = lax.rem(c, per_row)
        r = c // per_row + 1

        @pl.when(c == min(3, whole - 1) * per_row)
        def _():
            @pl.when(has_last)
            def _():
                halo(0).wait_recv()

            @pl.when(has_next)
            def _():
                halo(1).wait_recv()

            lat_row(rows - 1)
            send_row(rows - 1, 0)
            lat_row(0)
            send_row(0, 0)
            for group in range(1, groups):
                for k in range(SPLIT):
                    send_row((whole + 1 + k) % rows, group)

        wait_piece(r, b)
        remap_block(r, b, 0, count)
        heat_block(r, b)

    def tail_block(t):
        at = lax.rem(t, tail)
        return lax.rem(whole + 1 + at // per_row, rows), lax.rem(at, per_row), t // tail

    @pl.loop(0, groups * tail - 1)
    def _(t):
        r, b, group = tail_block(t)

        wait_piece(r, b, group)
        remap_block(r, b, group * LEAD, LEAD)

        @pl.when(group == 0)
        def _():
            heat_block(r, b)

        @pl.when(t == tail - 1)
        def _():
            @pl.loop(1, n_lat)
            def _(d):
                share_copy(d).start()

    end = per_row - 1
    carried[0:levels] = upper[0, end]

    landed(tbuf.at[:, pl.ds(0, depth * (n_lev - 1))], thick_send)

    @pl.when(has_next)
    def _():
        halo(0).wait_send()

    @pl.when(has_last)
    def _():
        halo(1).wait_send()

    others = gathered.at[pl.ds(1, n_lat - 1)]
    landed(others, share_recv)
    total = lax.fori_loop(1, n_lat, lambda d, total: total + gathered[d], shares[...])
    own = jnp.sum(jnp.where(lanes == lat, total, 0.0), axis=1, keepdims=True)
    carried[levels:] = jnp.broadcast_to(own, (8, BLOCK_COLS))
    landed(others, share_send)

    landed(sbuf.at[pl.ds(0, n_lev - 1)], send_sem)

    wait_piece(0, end, groups - 1)
    final[...] = rbuf[0, end, (groups - 1) * LEAD:groups * LEAD]


def store(
    moved, warm, final, carried, out, heating, owner_heat, tile, slope, above, owner, sems,
):
    count, rows, levels, piece = moved.shape
    rest = piece - BLOCK_COLS
    kept = count - LEAD
    owner[...] = carried[levels:levels + 1, 0:1]
    inner = pl.ds(1, rows - 1)
    pairs = [
        (moved.at[:, inner], out.at[:, inner]),
        (warm, heating),
        (owner, owner_heat),
        (moved.at[pl.ds(0, kept), 0], out.at[pl.ds(0, kept), 0]),
    ]
    if rest:
        pairs.append((
            moved.at[pl.ds(kept, LEAD), 0, :, pl.ds(0, rest)],
            out.at[pl.ds(kept, LEAD), 0, :, pl.ds(0, rest)],
        ))
    copies = [
        pltpu.make_async_copy(source, target, sems.at[k])
        for k, (source, target) in enumerate(pairs)
    ]
    for copy in copies:
        copy.start()

    def put(f, i, value):
        tile[f, i:i + TILE, :] = value

    remap(
        levels, carried[levels - 1:levels, :] / levels, lambda j, k: carried[j:k, :],
        lambda f, j, k: final[f, j:k, :], LEAD, put, slope, above,
    )
    last = pltpu.make_async_copy(
        tile, out.at[pl.ds(kept, LEAD), 0, :, pl.ds(rest, BLOCK_COLS)], sems.at[len(pairs)]
    )
    last.start()
    for copy in copies:
        copy.wait()
    last.wait()


def per_device(
    fields, thickness, courant_lon, courant_lat, exchange, solar_profile, owners, daylight
):
    n_lat, n_lev = lax.axis_size("lat"), lax.axis_size("lev")
    count, rows, depth, width = fields.shape
    levels = solar_profile.shape[0]
    piece = width // n_lev
    per_row = piece // BLOCK_COLS
    groups = count // LEAD
    f32 = jnp.float32
    dma = pltpu.SemaphoreType.DMA
    regular = pltpu.SemaphoreType.REGULAR
    hbm = pl.BlockSpec(memory_space=pltpu.HBM)
    vmem = pl.BlockSpec(memory_space=pltpu.VMEM)
    moved = jax.ShapeDtypeStruct((count, rows, levels, piece), f32)
    warm = jax.ShapeDtypeStruct((rows, levels, piece), f32)
    owner = jax.ShapeDtypeStruct((1, 1), f32)
    results = pl.pallas_call(
        functools.partial(kernel, n_lat, n_lev),
        out_shape=(
            pltpu.VMEM(moved.shape, f32),
            pltpu.VMEM(warm.shape, f32),
            pltpu.VMEM((LEAD, levels, BLOCK_COLS), f32),
            pltpu.VMEM((levels + 8, BLOCK_COLS), f32),
        ),
        in_specs=[hbm] * 8,
        out_specs=(vmem,) * 4,
        scratch_shapes=[
            pltpu.VMEM((count + 2, rows, depth, width), f32),
            pltpu.VMEM((count, rows + 2, depth, width), f32),
            pltpu.VMEM((n_lev, rows, per_row, count, depth, BLOCK_COLS), f32),
            pltpu.VMEM((rows, per_row, count, levels, BLOCK_COLS), f32),
            pltpu.VMEM((rows, levels, piece), f32),
            pltpu.VMEM(exchange.shape, f32),
            pltpu.VMEM((levels, 3 * exchange.shape[0] * levels), jnp.bfloat16),
            pltpu.VMEM((1, levels), f32),
            pltpu.VMEM((rows, per_row, levels, BLOCK_COLS), f32),
            pltpu.VMEM((count, levels, BLOCK_COLS), f32),
            pltpu.VMEM((levels, BLOCK_COLS), f32),
            pltpu.VMEM((1, BLOCK_COLS), f32),
            pltpu.VMEM((n_lat, 1, BLOCK_COLS), f32),
            pltpu.SMEM((rows * per_row,), jnp.int32),
            pltpu.SMEM((rows * per_row,), jnp.int32),
            regular,
            dma,
            dma((4,)),
            dma((2,)),
            dma((2,)),
            dma,
            dma,
            dma,
            dma(((rows - SPLIT + SPLIT * groups) * per_row,)),
            dma,
            dma,
        ],
        compiler_params=pltpu.CompilerParams(
            collective_id=0, has_side_effects=True, vmem_limit_bytes=61400000
        ),
    )(
        fields, thickness, courant_lon, courant_lat, exchange, solar_profile[None, :],
        owners[:, 0], daylight,
    )
    return pl.pallas_call(
        store,
        out_shape=(moved, warm, owner),
        in_specs=[vmem] * 4,
        out_specs=(hbm,) * 3,
        scratch_shapes=[
            pltpu.VMEM((LEAD, levels, BLOCK_COLS), f32),
            pltpu.VMEM((LEAD, levels, BLOCK_COLS), f32),
            pltpu.VMEM((levels, BLOCK_COLS), f32),
            pltpu.VMEM(owner.shape, f32),
            dma((6,)),
        ],
        compiler_params=pltpu.CompilerParams(vmem_limit_bytes=12 * 1024 * 1024),
    )(*results)


def solution(mesh):
    placed = (
        P(None, "lat", "lev", None),
        P("lat", "lev", None),
        P("lat", "lev", None),
        P("lat", "lev", None),
        P(),
        P(),
        P(("lat", "lev"), None),
        P(("lat", "lev")),
    )
    return jax.shard_map(
        per_device,
        mesh=mesh,
        in_specs=placed,
        out_specs=(P(None, "lat", None, "lev"), P("lat", None, "lev"), P("lat", "lev")),
        check_vma=False,
    )
```
